256 devices in a mesh: row: 32 (over z, y), col: 8 (over x, core).
Axes of the slice: x: 4, y: 4, z: 8, core: 2. Of those that a mesh axis runs over, the one named last changes fastest.
Arguments:
- feats: bfloat16 [131072, 256], P(('row', 'col')), may hold values from -6 to 6
- w_msg: bfloat16 [256, 256], replicated, may hold values from -0.375 to 0.375
- w_self: bfloat16 [256, 256], replicated, may hold values from -0.375 to 0.375
- bias: float32 [256], replicated, may hold values from -3 to 3
- hit_mask: int32 [131072], P(('row', 'col')), may hold values 0 or 1
- block_cols: int32 [32, 8, 96], P('row', 'col'), may hold values from 0 to 127, as said below
- block_count: int32 [32, 8], P('row', 'col'), may hold values from 32 to 96, as said below
- edge_vals: bfloat16 [32, 8, 96, 128, 128], P('row', 'col'), may hold values from -0.125 to 0.125
- grad_out: bfloat16 [131072, 256], P(('row', 'col')), may hold values from -3 to 3
Outputs:
- hidden: bfloat16 [131072, 256], P(('row', 'col'))
- grad_feats: bfloat16 [131072, 256], P(('row', 'col'))
- edge_grad: bfloat16 [32, 8, 96, 128, 128], P('row', 'col')
- w_msg_grad: float32 [256, 256], replicated
- w_self_grad: float32 [256, 256], replicated
- bias_grad: float32 [256], replicated
The draws below stay inside these ranges and needn't reach their ends.
Inputs may be any that keep to these rules, and one draw needn't show every extreme that they name: `block_cols`: slot s of a tile serves the tile's local block row s % 32; the block columns of the slots that serve one block row of one tile are different. Slots from block_count on are unused.
All inputs are finite; a program needn't handle non-finite values. No bound on the sum of `hit_mask` on one device may be relied on, other than what follows from the above.
Results may differ from the reference program's by a relative error of at most 0.015.
Values may be sent and summed in bfloat16 or wider, within the bound.
A program may use at most 128 MiB of HBM per device.

```python
import math
import jax
import jax.numpy as jnp
from jax import lax

F = 256
BLOCK = 128
HB = 4
K = 3
HITS = 131072
CAP = 96
N_ROW = 32
N_COL = 8


def slot_table(key):
    base = jax.random.fold_in(key, 17)
    key_near, key_far, key_count, key_top = jax.random.split(base, 4)
    tile_total = N_ROW * N_COL
    tile_rows = N_COL * HB
    tile_cols = N_ROW * HB
    block_total = HB * N_ROW * N_COL
    tile_index = jnp.arange(tile_total, dtype=jnp.int32)
    tile_row = tile_index // N_COL
    tile_col = tile_index % N_COL
    local_cols = jnp.arange(tile_cols, dtype=jnp.int32)
    global_rows = tile_row[:, None] * tile_rows + jnp.arange(tile_rows, dtype=jnp.int32)[None, :]
    global_cols = (local_cols[None, :] // HB * N_COL + tile_col[:, None]) * HB + local_cols[None, :] % HB
    spread = jnp.abs(global_cols[:, None, :] - global_rows[:, :, None])
    spread = jnp.minimum(spread, block_total - spread)
    near_noise = jax.random.randint(key_near, (tile_total, tile_rows, tile_cols), 0, 1024)
    near_score = jnp.where(spread <= 2 * tile_rows, 2097152, 0) + near_noise * 1024 + local_cols[None, None, :]
    first = lax.top_k(near_score, 1)[1].astype(jnp.int32)
    far_noise = jax.random.randint(key_far, (tile_total, tile_rows, tile_cols), 0, 1024)
    far_score = far_noise * 1024 + local_cols[None, None, :]
    far_score = jnp.where(local_cols[None, None, :] == first, -1, far_score)
    rest = lax.top_k(far_score, K - 1)[1].astype(jnp.int32)
    picks = jnp.concatenate([first, rest], axis=-1)
    slot_cols = jnp.transpose(picks, (0, 2, 1)).reshape(tile_total, CAP)
    slot_counts = jax.random.randint(key_count, (tile_total,), CAP // 3, CAP + 1)
    busiest = jax.random.randint(key_top, (), 0, tile_total)
    slot_counts = jnp.where(tile_index == busiest, CAP, slot_counts)
    slot_counts = jnp.where(tile_index == (busiest + 1) % tile_total, CAP // 3, slot_counts)
    return (slot_cols.astype(jnp.int32), slot_counts.astype(jnp.int32))


def draw_block_cols(key, part):
    slot_cols, slot_counts = slot_table(key)
    return slot_cols.reshape(N_ROW, N_COL, CAP).astype(jnp.int32)


def draw_block_count(key, part):
    slot_cols, slot_counts = slot_table(key)
    return slot_counts.reshape(N_ROW, N_COL).astype(jnp.int32)


def with_ends(values, own_key, least, largest):
    longest = values.shape.index(max(values.shape))
    spots = []
    for shift in (0, 1):
        where = [jax.random.randint(jax.random.fold_in(own_key, axis), (), 0, length) for axis, length in enumerate(values.shape)]
        where[longest] = (where[longest] + shift) % values.shape[longest]
        spots.append(tuple(where))
    return values.at[spots[0]].set(least).at[spots[1]].set(largest)


def level_of(key, extent, shards, low, top_value):
    gain = 1.0
    for position, blocks in shards:
        steps = jax.random.uniform(jax.random.fold_in(jax.random.fold_in(key, 6), position), (blocks,), jnp.float32, low / len(shards), top_value / len(shards))
        gain = gain * jnp.repeat(jnp.exp(steps), extent[position] // blocks).reshape((-1,) + (1,) * (len(extent) - 1 - position))
    return gain


def noise(own_key, shape, scale, reach, cuts=(), kind=jnp.bfloat16):
    level = level_of(own_key, shape, cuts, -0.22, 0.18) if cuts else 1.0
    array = jax.random.normal(own_key, shape, jnp.float32) * scale * level
    return jnp.minimum(jnp.maximum(array, -reach), reach).astype(kind)


def setup_inputs(seed: int = 0) -> dict:
    seeds = jax.random.split(jax.random.key(seed), 10)
    return {
        "feats": noise(seeds[0], (HITS, F), 1.0, 6.0, ((0, 256),)),
        "w_msg": noise(seeds[1], (F, F), F ** -0.5, 0.375),
        "w_self": noise(seeds[2], (F, F), F ** -0.5, 0.375),
        "bias": noise(seeds[3], (F,), 0.5, 3.0, (), jnp.float32),
        "hit_mask": with_ends((jax.random.randint(seeds[4], (HITS,), 0, 4) < 3).astype(jnp.int32), jax.random.fold_in(seeds[4], 1), 0, 1),
        "block_cols": draw_block_cols(jax.random.fold_in(seeds[9], 71), 0),
        "block_count": draw_block_count(jax.random.fold_in(seeds[9], 71), 0),
        "edge_vals": noise(seeds[7], (N_ROW, N_COL, CAP, BLOCK, BLOCK), (2 * K * N_COL * BLOCK // 3) ** -0.5, 0.125, ((0, 32), (1, 8))),
        "grad_out": noise(seeds[8], (HITS, F), 0.5, 3.0, ((0, 256),)),
    }


def reference(feats, w_msg, w_self, bias, hit_mask, block_cols, block_count, edge_vals, grad_out):
    row_mask = hit_mask.astype(jnp.float32)[:, None]
    messages = (jnp.dot(feats, w_msg, preferred_element_type=jnp.float32) * row_mask).astype(jnp.bfloat16)
    tile_rows = N_COL * HB
    tile_cols = N_ROW * HB
    msg_blocks = messages.reshape(HITS // BLOCK, BLOCK, F)
    slot_index = jnp.arange(CAP, dtype=jnp.int32)

    def tile_data(tile_row, tile_col):
        slot_cols = block_cols[tile_row, tile_col]
        slot_live = (slot_index < block_count[tile_row, tile_col]).astype(jnp.float32)
        edge_live = (edge_vals[tile_row, tile_col].astype(jnp.float32) * slot_live[:, None, None]).reshape(K, tile_rows, BLOCK, BLOCK)
        global_cols = ((slot_cols // HB * N_COL + tile_col) * HB + slot_cols % HB).astype(jnp.int32)
        col_blocks = msg_blocks[global_cols].astype(jnp.float32).reshape(K, tile_rows, BLOCK, F)
        return (slot_cols, slot_live, edge_live, col_blocks)

    def forward_tile(tile_row, tile_col):
        slot_cols, slot_live, edge_live, col_blocks = tile_data(tile_row, tile_col)
        return jnp.einsum('krij,krjf->rif', edge_live, col_blocks)

    def forward_row(tile_row):
        parts = lax.map(lambda tile_col: forward_tile(tile_row, tile_col), jnp.arange(N_COL, dtype=jnp.int32))
        return lax.optimization_barrier(jnp.sum(parts, axis=0))
    summed = lax.map(forward_row, jnp.arange(N_ROW, dtype=jnp.int32)).reshape(HITS, F)
    pre = summed + jnp.dot(feats, w_self, preferred_element_type=jnp.float32) + bias
    sig = jax.nn.sigmoid(pre)
    hidden = (pre * sig * row_mask).astype(jnp.bfloat16)
    deriv = sig * (1.0 + pre * (1.0 - sig))
    grad_pre = (grad_out.astype(jnp.float32) * row_mask * deriv).astype(jnp.bfloat16)
    grad_blocks = grad_pre.reshape(N_ROW, tile_rows, BLOCK, F)

    def backward_tile(tile_row, tile_col):
        slot_cols, slot_live, edge_live, col_blocks = tile_data(tile_row, tile_col)
        row_blocks = grad_blocks[tile_row].astype(jnp.float32)
        backward = jnp.einsum('krij,rif->krjf', edge_live, row_blocks).reshape(CAP, BLOCK, F)
        term = jax.ops.segment_sum(backward, slot_cols, num_segments=tile_cols).astype(jnp.bfloat16)
        edge_grad = (jnp.einsum('rif,krjf->krij', row_blocks, col_blocks).reshape(CAP, BLOCK, BLOCK) * slot_live[:, None, None]).astype(jnp.bfloat16)
        return (term, edge_grad)

    def backward_row(total, tile_row):
        terms, edge_grads = lax.map(lambda tile_col: backward_tile(tile_row, tile_col), jnp.arange(N_COL, dtype=jnp.int32))
        return (total + terms.astype(jnp.float32), edge_grads)
    start = jnp.zeros((N_COL, tile_cols, BLOCK, F), jnp.float32)
    total, edge_grad = lax.scan(backward_row, start, jnp.arange(N_ROW, dtype=jnp.int32))
    grad_sum = jnp.transpose(total.reshape(N_COL, N_ROW, HB, BLOCK, F), (1, 0, 2, 3, 4)).reshape(HITS, F)
    grad_msg = (grad_sum * row_mask).astype(jnp.bfloat16)
    grad_feats = (jnp.dot(grad_msg, w_msg.T, preferred_element_type=jnp.float32) + jnp.dot(grad_pre, w_self.T, preferred_element_type=jnp.float32)).astype(jnp.bfloat16)
    factor = 1.0 / math.sqrt(HITS)
    w_msg_grad = jnp.dot(feats.T, grad_msg, preferred_element_type=jnp.float32) * factor
    w_self_grad = jnp.dot(feats.T, grad_pre, preferred_element_type=jnp.float32) * factor
    bias_grad = lax.optimization_barrier(jnp.sum(grad_pre.astype(jnp.float32), axis=0)) * factor
    return (hidden, grad_feats, edge_grad, w_msg_grad, w_self_grad, bias_grad)
```

```python
import heapq
import math

import jax
import jax.numpy as jnp
from jax import lax
from jax.experimental import pallas as pl
from jax.experimental.pallas import tpu as pltpu
from jax.sharding import PartitionSpec as P

NZ, NY, NX, NC = 8, 4, 4, 8
OWN, FEAT, WIDE, BLK = 512, 256, 128, 128
CAP, TROWS, TCOLS = 96, 32, 128
CUT = 48
HALF = {1: (0, 2), -1: (2, 4)}
ALL = (0, 4)
FIDX, PERM, PROW, SAME, UIDX = 0, 96, 192, 288, 384
TABLE = 512
MESH = pl.DeviceIdType.MESH
BF, F32 = jnp.bfloat16, jnp.float32


def plane_messages():
    out = {}
    low, high = (0, CUT), (CUT, BLK)
    for d in (1, -1):
        out["PY1", d] = ("y", d, (), (0, -d), ALL, low)
        out["QZ", d, 1] = ("z", d, (), (-d, 0), ALL, high)
    for d in (1, -1):
        out["PZ", d, 1, 0] = ("z", d, (), (-d, 0), ALL, low)
        out["QY1", d, 0] = ("y", d, (), (0, -d), ALL, high)
    for d in (1, -1):
        out["PY2", d] = ("y", d, (("PY1", d),), (0, -2 * d), HALF[d], low)
    first = {-1: (("PY1", 1),), 1: (("PY1", -1),), 2: (("PY2", 1), ("PY2", -1))}
    for o in (0, -1, 1, 2):
        for d in (1, -1):
            for t in (1, 2, 3, 4):
                if (o, t) == (0, 1):
                    continue
                parents = first[o] if t == 1 else (("PZ", d, t - 1, o),)
                out["PZ", d, t, o] = ("z", d, parents, (-t * d, o), HALF[d] if t == 4 else ALL, low)
    for d in (1, -1):
        for t in (2, 3, 4):
            blocks = HALF[d] if t == 4 else ALL
            out["QZ", d, t] = ("z", d, (("QZ", d, t - 1),), (-t * d, 0), blocks, high)
    for oz in (0, -1, 1, -2, 2, -3, 3, 4):
        for d in (1, -1):
            if oz == 4:
                parents = (("QZ", 1, 4), ("QZ", -1, 4))
            else:
                parents = (("QZ", 1 if oz < 0 else -1, abs(oz)),)
            if oz:
                out["QY1", d, oz] = ("y", d, parents, (oz, -d), ALL, high)
            out["QY2", d, oz] = ("y", d, (("QY1", d, oz),), (oz, -2 * d), HALF[d], high)
    return out


def rows_in(message):
    (b0, b1), (lo, hi) = message[4:6]
    return (b1 - b0) * (hi - lo)


def plane_order(messages, second):
    rate, latency = 46e3, 1.7
    free, heap, got, order = {}, [], set(), []
    count = 0

    def issue(now, chunk, key):
        nonlocal count
        axis, d = messages[key][:2]
        start = max(now, free.get((axis, d), 0.0))
        free[axis, d] = start + rows_in(messages[key]) * WIDE * 2 / rate
        heapq.heappush(heap, (free[axis, d] + latency, count, chunk, key))
        count += 1

    def roots(now, chunk):
        for key, message in messages.items():
            if not message[2]:
                issue(now, chunk, key)

    roots(0.0, 0)
    heapq.heappush(heap, (second, -1, 1, None))
    while heap:
        now, _, chunk, key = heapq.heappop(heap)
        order.append((chunk, key, now))
        if key is None:
            roots(now, 1)
            continue
        got.add((chunk, key))
        for other, message in messages.items():
            if key in message[2] and all((chunk, p) in got for p in message[2]):
                issue(now, chunk, other)
    return order


MESSAGES = plane_messages()
ORDER = plane_order(MESSAGES, 20.0)
NUMBER = {key: i for i, key in enumerate(MESSAGES)}
COUNT = len(MESSAGES)
OFFSET = {}
_total = 0
for _key, _m in MESSAGES.items():
    OFFSET[_key] = _total
    _total += rows_in(_m)
PLANE_ROWS = _total
CHILDREN = {key: [k for k, m in MESSAGES.items() if key in m[2]] for key in MESSAGES}
ROOTS = [k for k, m in MESSAGES.items() if not m[2]]


def kernel(
    tab, bias, mask, feats, w_msg, w_self, gout, edges,
    hidden, gfeats, edge_out, wgrad, bgrad,
    F0, F1, A, AT, U0, U1, SS0, SS1, SR0, SR1, H0, H1, EB,
    XS0, XS1, XR0, XR1, CS, RX0, RX1, RR0, RR1, SO, SH, GP, GW,
    WC, WR, ZS, ZR, YR, ZG, CG,
    loc, ag_s, ag_r, rs_s, rs_r, x_s, x_r, h_s, h_r, w_s, w_r,
):
    F, U, SS, SR, H = (F0, F1), (U0, U1), (SS0, SS1), (SR0, SR1), (H0, H1)
    XS, XR, RX, RR = (XS0, XS1), (XR0, XR1), (RX0, RX1), (RR0, RR1)
    row = lax.axis_index("row")
    col = lax.axis_index("col")
    z, y = row // NY, row % NY
    x, core = col // 2, col % 2
    other = 1 - core
    sent = []

    def plane_device(dz, dy):
        return ((z + dz) % NZ * NY + (y + dy) % NY, col)

    def col_device(dx, swap=False):
        return (row, (x + dx) % NX * 2 + (other if swap else core))

    def remote(src, dst, ssem, rsem, device):
        return pltpu.make_async_remote_copy(
            src_ref=src, dst_ref=dst, send_sem=ssem, recv_sem=rsem,
            device_id=device, device_id_type=MESH,
        )

    def begin(copy):
        copy.start()
        sent.append(copy)

    def rows_of(start, size, step=16):
        return pl.ds(pl.multiple_of(start, step), size)

    edge_in = pltpu.make_async_copy(edges, A, loc.at[0])
    edge_in.start()
    fm = feats[...] * mask[...].astype(BF)
    for c in (0, 1):
        for n in range(4):
            F[c][row * 4 + n] = fm[n * BLK:(n + 1) * BLK, c * WIDE:(c + 1) * WIDE]
        F[c][TCOLS] = jnp.zeros((BLK, WIDE), BF)
        U[c][CAP] = jnp.zeros((BLK, WIDE), BF)

    barrier = pltpu.get_barrier_semaphore()
    peers = [plane_device(0, d) for d in range(1, NY)]
    peers += [plane_device(d, 0) for d in range(1, NZ)]
    peers += [(row, (col + d) % NC) for d in range(1, NC)]
    for peer in peers:
        pl.semaphore_signal(barrier, inc=1, device_id=peer, device_id_type=MESH)
    pl.semaphore_wait(barrier, len(peers))

    gathers = {}

    def gather_copy(c, key):
        if (c, key) not in gathers:
            axis, d, _, (dz, dy), (b0, b1), (lo, hi) = MESSAGES[key]
            sz, sy = (dz + d, dy) if axis == "z" else (dz, dy + d)
            block = (z + sz) % NZ * NY + (y + sy) % NY
            part = F[c].at[pl.ds(block * 4 + b0, b1 - b0), pl.ds(lo, hi - lo), :]
            i = c * COUNT + NUMBER[key]
            target = plane_device(d, 0) if axis == "z" else plane_device(0, d)
            gathers[c, key] = remote(part, part, ag_s.at[i], ag_r.at[i], target)
        return gathers[c, key]

    def transpose_slot(j):
        def run():
            AT[j] = A[tab[0, PERM + j]].astype(F32).T.astype(BF)
        return run

    def sum_block(c, owner, j, dest, place):
        l = owner * 4 + j
        acc = None
        for k in range(3):
            s = k * TROWS + l
            d = jnp.dot(A[s], F[c][tab[0, FIDX + s]], preferred_element_type=F32)
            acc = d if acc is None else acc + d
        dest[rows_of(place * OWN + j * BLK, BLK, BLK), :] = acc.astype(dest.dtype)

    swaps = {}

    def swap_copy(c, xi):
        if (c, xi) not in swaps:
            part = pl.ds(xi * OWN, OWN)
            swaps[c, xi] = remote(
                XS[c].at[part, :], XR[c].at[part, :],
                x_s.at[c * 8 + xi], x_r.at[c * 8 + xi], col_device(0, True),
            )
        return swaps[c, xi]

    rings = {}
    RING = {("X1", 1): (0, 512), ("X1", -1): (512, 512), ("X2", 1): (1024, 256), ("X2", -1): (1280, 256)}

    def ring_copy(c, key):
        if (c, key) not in rings:
            lo, size = RING[key]
            i = c * 8 + 4 + list(RING).index(key)
            rings[c, key] = remote(
                RX[c].at[pl.ds(lo, size), :], RR[c].at[pl.ds(lo, size), :],
                x_s.at[i], x_r.at[i], col_device(-key[1]),
            )
        return rings[c, key]

    def chip_sum(c, xi, lo, size):
        part = rows_of(xi * OWN + lo, size)
        return CS[part, :] + XR[c][part, :].astype(F32)

    def ring_far(c):
        for xi in range(NX):
            swap_copy(c, xi).wait_recv()
        for d in (1, -1):
            lo, size = RING["X2", d]
            RX[c][pl.ds(lo, size), :] = chip_sum(
                c, (x + 2) % NX, 0 if d > 0 else 256, 256
            ).astype(BF)
            begin(ring_copy(c, ("X2", d)))

    def ring_near(c):
        for d in (1, -1):
            ring_copy(c, ("X2", d)).wait_recv()
            lo = RING["X1", d][0]
            came = RING["X2", d][0]
            to = (x - d) % NX
            for part in (0, 1):
                value = chip_sum(c, to, part * 256, 256)
                if part == (0 if d > 0 else 1):
                    value = value + RR[c][pl.ds(came, 256), :].astype(F32)
                RX[c][pl.ds(lo + part * 256, 256), :] = value.astype(BF)
            begin(ring_copy(c, ("X1", d)))

    def ring_end(c):
        for d in (1, -1):
            ring_copy(c, ("X1", d)).wait_recv()
        SO[:, c * WIDE:(c + 1) * WIDE] = (
            chip_sum(c, x, 0, OWN)
            + RR[c][pl.ds(0, 512), :].astype(F32)
            + RR[c][pl.ds(512, 512), :].astype(F32)
        )

    def sum_slot(c, n):
        def run():
            xi, j = n % 16 // 4, n % 4
            if n < 16:
                sum_block(c, 2 * xi + other, j, XS[c], xi)
                if j == 3:
                    begin(swap_copy(c, xi))
            else:
                sum_block(c, 2 * xi + core, j, CS, xi)
        return run

    for key in ROOTS:
        begin(gather_copy(0, key))
    arrived = set()
    fillers = [edge_in.wait] + [transpose_slot(j) for j in range(CAP)]
    ends = 0
    for chunk, key, _ in ORDER:
        if key is None:
            for root in ROOTS:
                begin(gather_copy(1, root))
            continue
        gather_copy(chunk, key).wait_recv()
        arrived.add((chunk, key))
        for nxt in CHILDREN[key]:
            if all((chunk, p) in arrived for p in MESSAGES[nxt][2]):
                begin(gather_copy(chunk, nxt))
        if chunk == 0 and sum(1 for c, _k in arrived if c == 0) == COUNT:
            fillers += [sum_slot(0, n) for n in range(32)]
            fillers += [None] * 4 + [lambda: ring_far(0)]
            fillers += [None] * 8 + [lambda: ring_near(0)]
        done = 0
        while fillers and done < (1 if ends else 2):
            f = fillers.pop(0)
            done += 1
            if f is not None:
                f()
    for f in fillers:
        if f is not None:
            f()
    ring_end(0)

    @pl.loop(0, 4)
    def _(xi):
        for j in range(4):
            sum_block(1, 2 * xi + other, j, XS[1], xi)

    for xi in range(NX):
        begin(swap_copy(1, xi))

    @pl.loop(0, 4)
    def _(xi):
        for j in range(4):
            sum_block(1, 2 * xi + core, j, CS, xi)

    ring_far(1)
    ring_near(1)
    ring_end(1)

    T_DIM = (((1,), (1,)), ((), ()))
    C_DIM = (((0,), (0,)), ((), ()))

    @pl.loop(0, 4)
    def _(i):
        part = rows_of(i * BLK, BLK, BLK)
        s = SO[part, :]
        hi = s.astype(BF)
        lo = (s - hi.astype(F32)).astype(BF)
        SH[part, :] = hi
        mine = row * 4 + i
        pre = jnp.dot(hi, w_msg[...], preferred_element_type=F32)
        pre += jnp.dot(lo, w_msg[...], preferred_element_type=F32)
        pre += jnp.dot(F0[mine], w_self[:WIDE, :], preferred_element_type=F32)
        pre += jnp.dot(F1[mine], w_self[WIDE:, :], preferred_element_type=F32)
        pre += bias[...]
        real = mask[part, :]
        sig = jax.nn.sigmoid(pre)
        hidden[part, :] = (pre * sig * real).astype(BF)
        deriv = sig * (1.0 + pre * (1.0 - sig))
        gp = (gout[part, :].astype(F32) * real * deriv).astype(BF)
        GP[part, :] = gp
        h = lax.dot_general(gp, w_msg[...], T_DIM, preferred_element_type=F32).astype(BF)
        H0[col * 4 + i] = h[:, :WIDE]
        H1[col * 4 + i] = h[:, WIDE:]

    shares = {}
    SHARE = {
        ("X1", 1): (0, 1, False, -1, 0, 4), ("X1", -1): (1, -1, False, 1, 0, 4),
        ("X2", 1): (2, 1, False, -2, 0, 2), ("X2", -1): (3, -1, False, 2, 2, 2),
        ("S", 0): (4, 0, True, 0, 0, 4), ("S", -1): (5, 0, True, -1, 0, 4),
        ("S", 1): (6, 0, True, 1, 0, 4),
        ("S", 2): (7, 0, True, 2, 0, 2), ("S", 3): (8, 0, True, 2, 2, 2),
    }

    def share_copy(c, key):
        if (c, key) not in shares:
            i, dx, swap, origin, lo, size = SHARE[key]
            from_x = origin if swap else origin + dx
            block = (x + from_x) % NX * 2 + core
            part = H[c].at[pl.ds(block * 4 + lo, size)]
            i += 9 * c
            shares[c, key] = remote(part, part, h_s.at[i], h_r.at[i], col_device(dx, swap))
        return shares[c, key]

    def share_start(c):
        for key in (("X1", 1), ("X1", -1), ("S", 0)):
            begin(share_copy(c, key))

    def share_near(c):
        for d in (1, -1):
            share_copy(c, ("X1", d)).wait_recv()
            begin(share_copy(c, ("X2", d)))
            begin(share_copy(c, ("S", -d)))

    def share_far(c):
        for d in (1, -1):
            share_copy(c, ("X2", d)).wait_recv()
            begin(share_copy(c, ("S", 2 if d > 0 else 3)))

    def share_end(c):
        for n in (0, -1, 1, 2, 3):
            share_copy(c, ("S", n)).wait_recv()

    def term_slots(c, start, count, acc):
        def body(n, acc):
            for u in range(4):
                j = start + n * 4 + u
                h = H[c][tab[0, PROW + j]]
                at = AT[j]
                keep = tab[0, SAME + j].astype(F32)
                acc = acc * keep + jnp.dot(at, h, preferred_element_type=F32)
                U[c][j] = acc.astype(BF)
            return acc
        return lax.fori_loop(0, count // 4, body, acc)

    share_start(0)
    share_start(1)

    WG = WC

    @pl.loop(0, 1)
    def _(i):
        gp = GP[...]
        w1 = lax.dot_general(SH[...], gp, C_DIM, preferred_element_type=F32)
        for n in range(4):
            WG[n, 0:64, :] = w1[n * 64:(n + 1) * 64]
        for c in (0, 1):
            fc = F[c][pl.ds(row * 4, 4)].reshape(OWN, WIDE)
            w2 = lax.dot_general(fc, gp, C_DIM, preferred_element_type=F32)
            for n in range(2):
                WG[4 + 2 * c + n, 0:64, :] = w2[n * 64:(n + 1) * 64]
        b = jnp.sum(gp.astype(F32).reshape(64, 8, FEAT), axis=0)
        for n in range(8):
            WG[n, 64:72, :] = b
        GW[...] = lax.dot_general(gp, w_self[...], T_DIM, preferred_element_type=F32)

    share_near(0)
    share_far(0)
    share_near(1)
    share_end(0)
    zero = jnp.zeros((BLK, WIDE), F32)
    term_slots(0, 0, CAP, zero)

    stages = {}

    def stage_copy(kind, d):
        if (kind, d) not in stages:
            if kind == "col":
                to = (col + d) % NC
                stages[kind, d] = remote(
                    WC.at[to], WR.at[col], w_s.at[d], w_r.at[d], (row, to))
            elif kind == "z":
                to = (z + d) % NZ
                stages[kind, d] = remote(
                    ZS.at[to], ZR.at[z], w_s.at[8 + d], w_r.at[8 + d], plane_device(d, 0))
            elif kind == "y":
                stages[kind, d] = remote(
                    YR.at[y], YR.at[y], w_s.at[16 + d], w_r.at[16 + d], plane_device(0, d))
            elif kind == "zg":
                stages[kind, d] = remote(
                    ZG.at[z], ZG.at[z], w_s.at[20 + d], w_r.at[20 + d], plane_device(d, 0))
            else:
                to = (col + d) % NC
                stages[kind, d] = remote(
                    CG.at[col], CG.at[col], w_s.at[28 + d], w_r.at[28 + d], (row, to))
        return stages[kind, d]

    def stage_send(kind, n):
        for d in range(1, n):
            begin(stage_copy(kind, d))

    def stage_wait(kind, n):
        for d in range(1, n):
            stage_copy(kind, d).wait_recv()

    def weights_0():
        WR[col] = WC[col]
        stage_send("col", NC)

    def weights_1():
        stage_wait("col", NC)
        v = WR[0]
        for n in range(1, NC):
            v = v + WR[n]
        for n in range(NZ):
            ZS[n, 0:8, :] = v[n * 8:n * 8 + 8]
            ZS[n, 8:16, :] = v[64:72]
        ZR[z] = ZS[z]
        stage_send("z", NZ)

    def weights_2():
        stage_wait("z", NZ)
        v = ZR[0]
        for n in range(1, NZ):
            v = v + ZR[n]
        YR[y] = v
        stage_send("y", NY)

    def weights_3():
        stage_wait("y", NY)
        v = (YR[0] + YR[1]) + (YR[2] + YR[3])
        ZG[z] = v[0:8]
        bgrad[...] = v[8:16]
        stage_send("zg", NZ)

    def weights_4():
        stage_wait("zg", NZ)
        for n in range(NZ):
            CG[col, n * 8:n * 8 + 8, :] = ZG[n]
        stage_send("cg", NC)

    def weights_5():
        stage_wait("cg", NC)
        for n in range(NC):
            wgrad[n * 64:(n + 1) * 64, :] = CG[n]

    reduces = {}

    def reduce_copy(c, key):
        if (c, key) not in reduces:
            axis, d = MESSAGES[key][:2]
            part = pl.ds(OFFSET[key], rows_in(MESSAGES[key]))
            i = c * COUNT + NUMBER[key]
            target = plane_device(-d, 0) if axis == "z" else plane_device(0, -d)
            reduces[c, key] = remote(
                SS[c].at[part, :], SR[c].at[part, :], rs_s.at[i], rs_r.at[i], target)
        return reduces[c, key]

    def total_piece(c, block, n, lo, hi, children):
        value = U[c][tab[0, UIDX + block * 4 + n], lo:hi, :].astype(F32)
        for k in children:
            (b0, b1), rows = MESSAGES[k][4:6]
            if rows == (lo, hi) and b0 <= n < b1:
                at = OFFSET[k] + (n - b0) * (hi - lo)
                value = value + SR[c][pl.ds(at, hi - lo), :].astype(F32)
        return value

    waited = set()

    def reduce_wait(c, keys):
        for k in keys:
            if (c, k) not in waited:
                waited.add((c, k))
                reduce_copy(c, k).wait_recv()

    def reduce_send(c, key):
        _, _, _, (dz, dy), (b0, b1), (lo, hi) = MESSAGES[key]
        children = CHILDREN[key]
        reduce_wait(c, children)
        block = (z + dz) % NZ * NY + (y + dy) % NY
        for n in range(b0, b1):
            at = OFFSET[key] + (n - b0) * (hi - lo)
            SS[c][pl.ds(at, hi - lo), :] = total_piece(c, block, n, lo, hi, children).astype(BF)
        begin(reduce_copy(c, key))

    def finish(c):
        reduce_wait(c, ROOTS)
        part = slice(c * WIDE, (c + 1) * WIDE)
        for n in range(4):
            for lo, hi in ((0, CUT), (CUT, BLK)):
                a, b = n * BLK + lo, n * BLK + hi
                value = total_piece(c, row, n, lo, hi, ROOTS) * mask[a:b, :]
                gfeats[a:b, part] = (value + GW[a:b, part]).astype(BF)

    def edge_slot(s):
        def run():
            e = None
            for c in (0, 1):
                f = F[c][tab[0, FIDX + s]]
                d = lax.dot_general(H[c][s % TROWS], f, T_DIM, preferred_element_type=F32)
                e = d if e is None else e + d
            EB[s] = e.astype(BF)
        return run

    plan = [(1 - chunk, key) for chunk, key, _ in reversed(ORDER) if key is not None]
    later = next(i for i, (c, _) in enumerate(plan) if c == 1)
    steps = {16: weights_0, 56: weights_1}
    acc = zero
    edge_work = []
    for i, (c, key) in enumerate(plan):
        if i == later - 12:
            share_far(1)
        if i == later:
            share_end(1)
            term_slots(1, 0, CAP, zero)
            edge_work = [edge_slot(s) for s in range(CAP)]
        reduce_send(c, key)
        if i in steps:
            steps[i]()
        if i > later + 8:
            for _ in range(2):
                if edge_work:
                    edge_work.pop(0)()
        if i == later + 14:
            weights_2()
        if i == later + 26:
            weights_3()
        if i == later + 38:
            weights_4()
        if i == later + 54:
            weights_5()
    for f in edge_work:
        f()
    edge_copy = pltpu.make_async_copy(EB, edge_out, loc.at[1])
    edge_copy.start()
    finish(0)
    finish(1)
    for copy in sent:
        copy.wait_send()
    edge_copy.wait()


def run_kernel(tab, bias, mask, feats, w_msg, w_self, gout, edges):
    vm = pl.BlockSpec(memory_space=pltpu.VMEM)
    dma = pltpu.SemaphoreType.DMA
    b16 = lambda rows: pltpu.VMEM((rows, WIDE), BF)
    f32 = lambda *shape: pltpu.VMEM(shape, F32)
    blocks = lambda n: pltpu.VMEM((n, BLK, WIDE), BF)
    edge_shape = jax.ShapeDtypeStruct((CAP, BLK, BLK), BF)
    scratch = [
        blocks(TCOLS + 1), blocks(TCOLS + 1), blocks(CAP), blocks(CAP),
        blocks(CAP + 1), blocks(CAP + 1),
        b16(PLANE_ROWS), b16(PLANE_ROWS), b16(PLANE_ROWS), b16(PLANE_ROWS),
        blocks(TROWS), blocks(TROWS), blocks(CAP),
        b16(NX * OWN), b16(NX * OWN), b16(NX * OWN), b16(NX * OWN), f32(NX * OWN, WIDE),
        b16(1536), b16(1536), b16(1536), b16(1536),
        f32(OWN, FEAT), pltpu.VMEM((OWN, FEAT), BF), pltpu.VMEM((OWN, FEAT), BF), f32(OWN, FEAT),
        f32(NC, 72, FEAT), f32(NC, 72, FEAT), f32(NZ, 16, FEAT), f32(NZ, 16, FEAT),
        f32(NY, 16, FEAT), f32(NZ, 8, FEAT), f32(NC, 64, FEAT),
        dma((2,)), dma((2 * COUNT,)), dma((2 * COUNT,)), dma((2 * COUNT,)), dma((2 * COUNT,)),
        dma((16,)), dma((16,)), dma((18,)), dma((18,)), dma((36,)), dma((36,)),
    ]
    return pl.pallas_call(
        kernel,
        out_shape=(
            jax.ShapeDtypeStruct((OWN, FEAT), BF),
            jax.ShapeDtypeStruct((OWN, FEAT), BF),
            edge_shape,
            jax.ShapeDtypeStruct((2 * FEAT, FEAT), F32),
            jax.ShapeDtypeStruct((8, FEAT), F32),
        ),
        in_specs=[pl.BlockSpec(memory_space=pltpu.SMEM)] + [vm] * 6
        + [pl.BlockSpec(memory_space=pl.ANY)],
        out_specs=(vm, vm, pl.BlockSpec(memory_space=pl.ANY), vm, vm),
        scratch_shapes=scratch,
        compiler_params=pltpu.CompilerParams(
            collective_id=0, has_side_effects=True, vmem_limit_bytes=64 * 1024 * 1024 - 65536
        ),
    )(tab, bias, mask, feats, w_msg, w_self, gout, edges)


def slot_tables(cols, count):
    s = jnp.arange(CAP, dtype=jnp.int32)
    key = jnp.where(s < count, cols, TCOLS)
    below = (key[None, :] < key[:, None]) | ((key[None, :] == key[:, None]) & (s[None, :] < s[:, None]))
    rank = jnp.sum(below.astype(jnp.int32), axis=1)
    place = (rank[None, :] == s[:, None]).astype(jnp.int32)
    perm = jnp.sum(place * s[None, :], axis=1)
    near = (key[None, :] == key[:, None]) & (s[None, :] < s[:, None])
    again = jnp.any(near, axis=1).astype(jnp.int32)
    same = jnp.sum(place * again[None, :], axis=1)
    m = jnp.arange(TCOLS, dtype=jnp.int32)
    last = jnp.sum((key[None, :] <= m[:, None]).astype(jnp.int32), axis=1) - 1
    has = jnp.any(key[None, :] == m[:, None], axis=1)
    uidx = jnp.where(has, last, CAP)
    return jnp.concatenate([key, perm, perm % TROWS, same, uidx])[None, :]


def per_device(feats, w_msg, w_self, bias, hit_mask, block_cols, block_count, edge_vals, grad_out):
    tab = slot_tables(block_cols[0, 0], block_count[0, 0])
    hidden, gfeats, edge, wgrad, bgrad = run_kernel(
        tab, bias[None, :], hit_mask.astype(F32)[:, None], feats, w_msg, w_self, grad_out,
        edge_vals.reshape(CAP, BLK, BLK),
    )
    factor = 1.0 / math.sqrt(OWN * NZ * NY * NC)
    return (
        hidden,
        gfeats,
        edge.reshape(1, 1, CAP, BLK, BLK),
        wgrad[:FEAT] * factor,
        wgrad[FEAT:] * factor,
        jnp.sum(bgrad, axis=0) * factor,
    )


def solution(mesh):
    placed = (
        P(("row", "col"), None),
        P(),
        P(),
        P(),
        P(("row", "col")),
        P("row", "col", None),
        P("row", "col"),
        P("row", "col", None, None, None),
        P(("row", "col"), None),
    )
    return jax.shard_map(
        per_device,
        mesh=mesh,
        in_specs=placed,
        out_specs=(
            P(("row", "col"), None),
            P(("row", "col"), None),
            P("row", "col", None, None, None),
            P(),
            P(),
            P(),
        ),
        check_vma=False,
    )
```

```python
import heapq
import math

import jax
import jax.numpy as jnp
from jax import lax
from jax.experimental import pallas as pl
from jax.experimental.pallas import tpu as pltpu
from jax.sharding import PartitionSpec as P

NZ, NY, NX, NC = 8, 4, 4, 8
OWN, FEAT, WIDE, BLK = 512, 256, 128, 128
CAP, TROWS, TCOLS = 96, 32, 128
CUT = 48
HALF = {1: (0, 2), -1: (2, 4)}
ALL = (0, 4)
FIDX, PERM, PROW, SAME, UIDX = 0, 96, 192, 288, 384
TABLE = 512
MESH = pl.DeviceIdType.MESH
FACTOR = 1.0 / math.sqrt(OWN * NZ * NY * NC)
BF, F32 = jnp.bfloat16, jnp.float32


def plane_messages():
    out = {}
    low, high = (0, CUT), (CUT, BLK)
    for d in (1, -1):
        out["PY1", d] = ("y", d, (), (0, -d), ALL, low)
        out["QZ", d, 1] = ("z", d, (), (-d, 0), ALL, high)
    for d in (1, -1):
        out["PZ", d, 1, 0] = ("z", d, (), (-d, 0), ALL, low)
        out["QY1", d, 0] = ("y", d, (), (0, -d), ALL, high)
    for d in (1, -1):
        out["PY2", d] = ("y", d, (("PY1", d),), (0, -2 * d), HALF[d], low)
    first = {-1: (("PY1", 1),), 1: (("PY1", -1),), 2: (("PY2", 1), ("PY2", -1))}
    for o in (0, -1, 1, 2):
        for d in (1, -1):
            for t in (1, 2, 3, 4):
                if (o, t) == (0, 1):
                    continue
                parents = first[o] if t == 1 else (("PZ", d, t - 1, o),)
                out["PZ", d, t, o] = ("z", d, parents, (-t * d, o), HALF[d] if t == 4 else ALL, low)
    for d in (1, -1):
        for t in (2, 3, 4):
            blocks = HALF[d] if t == 4 else ALL
            out["QZ", d, t] = ("z", d, (("QZ", d, t - 1),), (-t * d, 0), blocks, high)
    for oz in (0, -1, 1, -2, 2, -3, 3, 4):
        for d in (1, -1):
            if oz == 4:
                parents = (("QZ", 1, 4), ("QZ", -1, 4))
            else:
                parents = (("QZ", 1 if oz < 0 else -1, abs(oz)),)
            if oz:
                out["QY1", d, oz] = ("y", d, parents, (oz, -d), ALL, high)
            out["QY2", d, oz] = ("y", d, (("QY1", d, oz),), (oz, -2 * d), HALF[d], high)
    return out


def rows_in(message):
    (b0, b1), (lo, hi) = message[4:6]
    return (b1 - b0) * (hi - lo)


def plane_order(messages):
    rate, latency, ahead = 46e3, 1.7, 2.0
    took = {key: rows_in(m) * WIDE * 2 / rate for key, m in messages.items()}
    children = {key: [k for k, m in messages.items() if key in m[2]] for key in messages}
    weight = {}

    def path(key):
        if key not in weight:
            weight[key] = took[key] + latency + max([path(k) for k in children[key]] + [0.0])
        return weight[key]

    links = {m[:2]: 0.0 for m in messages.values()}
    ready = {link: [] for link in links}
    got, program, flying = set(), [], []

    def offer(chunk, key):
        heapq.heappush(ready[messages[key][:2]], (chunk, -path(key), NUMBER[key], key))

    for chunk in (0, 1):
        for key, m in messages.items():
            if not m[2]:
                offer(chunk, key)
    now = 0.0
    while True:
        while flying and flying[0][0] <= now + 1e-9:
            _, _, chunk, key = heapq.heappop(flying)
            program.append((False, chunk, key))
            got.add((chunk, key))
            for k in children[key]:
                if all((chunk, p) in got for p in messages[k][2]):
                    offer(chunk, k)
        for link in links:
            while ready[link] and links[link] - ahead <= now + 1e-9:
                chunk, _, number, key = heapq.heappop(ready[link])
                links[link] = max(now, links[link]) + took[key]
                heapq.heappush(flying, (links[link] + latency, len(program), chunk, key))
                program.append((True, chunk, key))
        times = [f[0] for f in flying[:1]] + [links[k] - ahead for k in links if ready[k]]
        if not times:
            return program, now
        now = max(now, min(times))


MESSAGES = plane_messages()
NUMBER = {key: i for i, key in enumerate(MESSAGES)}
PROGRAM, SPAN = plane_order(MESSAGES)
ORDER = [(chunk, key) for is_send, chunk, key in PROGRAM if not is_send]
TWIN = {key: (key[0], -key[1]) + key[2:] for key in MESSAGES}
PAIR = {key: NUMBER[key if key[1] > 0 else TWIN[key]] for key in MESSAGES}
COUNT = len(MESSAGES)
OFFSET = {}
_total = 0
for _key, _m in MESSAGES.items():
    OFFSET[_key] = _total
    _total += rows_in(_m)
PLANE_ROWS = _total
SLOT = {key: sorted(set(PAIR.values())).index(PAIR[key]) for key in MESSAGES}
CHILDREN = {key: [k for k, m in MESSAGES.items() if key in m[2]] for key in MESSAGES}
ROOTS = [k for k, m in MESSAGES.items() if not m[2]]


def kernel(
    tab, bias, mask, feats, w_msg, w_self, gout, edges,
    hidden, gfeats, edge_out, wgrad, bgrad,
    F0, F1, A, AT, U0, U1, SS0, SS1, SR0, SR1, H0, H1, EB,
    XS0, XS1, XR0, XR1, CS, RX0, RX1, RR0, RR1, SO, SH, GP, GW,
    WC, WR, ZS, ZR, YR, ZG, CG, ACC,
    loc, ag_s, ag_r, rs_s, rs_r, x_s, x_r, h_s, h_r, w_s, w_r,
):
    F, U, SS, SR, H = (F0, F1), (U0, U1), (SS0, SS1), (SR0, SR1), (H0, H1)
    XS, XR, RX, RR = (XS0, XS1), (XR0, XR1), (RX0, RX1), (RR0, RR1)
    row = lax.axis_index("row")
    col = lax.axis_index("col")
    z, y = row // NY, row % NY
    x, core = col // 2, col % 2
    other = 1 - core
    sent = []

    def plane_device(dz, dy):
        return ((z + dz) % NZ * NY + (y + dy) % NY, col)

    def col_device(dx, swap=False):
        return (row, (x + dx) % NX * 2 + (other if swap else core))

    def remote(src, dst, ssem, rsem, device):
        return pltpu.make_async_remote_copy(
            src_ref=src, dst_ref=dst, send_sem=ssem, recv_sem=rsem,
            device_id=device, device_id_type=MESH,
        )

    def begin(copy):
        copy.start()
        sent.append(copy)

    def rows_of(start, size, step=16):
        return pl.ds(pl.multiple_of(start, step), size)

    edge_in = pltpu.make_async_copy(edges, A, loc.at[0])
    edge_in.start()
    fm = feats[...] * mask[...].astype(BF)
    for c in (0, 1):
        for n in range(4):
            F[c][row * 4 + n] = fm[n * BLK:(n + 1) * BLK, c * WIDE:(c + 1) * WIDE]
        F[c][TCOLS] = jnp.zeros((BLK, WIDE), BF)
        U[c][CAP] = jnp.zeros((BLK, WIDE), BF)

    barrier = pltpu.get_barrier_semaphore()
    peers = [plane_device(0, d) for d in range(1, NY)]
    peers += [plane_device(d, 0) for d in range(1, NZ)]
    peers += [(row, (col + d) % NC) for d in range(1, NC)]
    for peer in peers:
        pl.semaphore_signal(barrier, inc=1, device_id=peer, device_id_type=MESH)
    pl.semaphore_wait(barrier, len(peers))

    gathers = {}

    def gather_copy(c, key):
        if (c, key) not in gathers:
            axis, d, _, (dz, dy), (b0, b1), (lo, hi) = MESSAGES[key]
            sz, sy = (dz + d, dy) if axis == "z" else (dz, dy + d)
            block = (z + sz) % NZ * NY + (y + sy) % NY
            part = F[c].at[pl.ds(block * 4 + b0, b1 - b0), pl.ds(lo, hi - lo), :]
            target = plane_device(d, 0) if axis == "z" else plane_device(0, d)
            gathers[c, key] = remote(part, part, ag_s.at[c], ag_r.at[c, SLOT[key]], target)
        return gathers[c, key]

    def pair_wait(c, sem, key):
        part = SR[c].at[pl.ds(0, 2 * rows_in(MESSAGES[key])), :]
        pltpu.make_async_copy(part, part, sem.at[c, SLOT[key]]).wait()

    def transpose_slot(j):
        def run():
            AT[j] = A[tab[0, PERM + j]].astype(F32).T.astype(BF)
        return run

    def sum_block(c, owner, j, dest, place):
        l = owner * 4 + j
        acc = None
        for k in range(3):
            s = k * TROWS + l
            d = jnp.dot(A[s], F[c][tab[0, FIDX + s]], preferred_element_type=F32)
            acc = d if acc is None else acc + d
        dest[rows_of(place * OWN + j * BLK, BLK, BLK), :] = acc.astype(dest.dtype)

    swaps = {}

    def swap_copy(c, xi):
        if (c, xi) not in swaps:
            part = pl.ds(xi * OWN, OWN)
            swaps[c, xi] = remote(
                XS[c].at[part, :], XR[c].at[part, :],
                x_s.at[c * 10 + xi], x_r.at[c * 10 + xi], col_device(0, True),
            )
        return swaps[c, xi]

    rings = {}
    RING = {
        ("F", 1): (0, 256), ("F", -1): (256, 256), ("E", 1): (512, 256), ("E", -1): (768, 256),
        ("L", 1): (1024, 256), ("L", -1): (1280, 256),
    }

    def ring_copy(c, key):
        if (c, key) not in rings:
            lo, size = RING[key]
            i = c * 10 + 4 + list(RING).index(key)
            rings[c, key] = remote(
                RX[c].at[pl.ds(lo, size), :], RR[c].at[pl.ds(lo, size), :],
                x_s.at[i], x_r.at[i], col_device(-key[1]),
            )
        return rings[c, key]

    def chip_sum(c, xi, lo, size):
        part = rows_of(xi * OWN + lo, size)
        return CS[part, :] + XR[c][part, :].astype(F32)

    def ring_far(c):
        for n in range(4):
            swap_copy(c, n).wait_recv()
        for d in (1, -1):
            lo, size = RING["F", d]
            RX[c][pl.ds(lo, size), :] = chip_sum(
                c, (x + 2) % NX, 0 if d > 0 else 256, 256).astype(BF)
            begin(ring_copy(c, ("F", d)))
        for d in (1, -1):
            lo, size = RING["E", d]
            RX[c][pl.ds(lo, size), :] = chip_sum(
                c, (x - d) % NX, 256 if d > 0 else 0, 256).astype(BF)
            begin(ring_copy(c, ("E", d)))

    def ring_near(c):
        for d in (1, -1):
            ring_copy(c, ("F", d)).wait_recv()
            lo, size = RING["L", d]
            value = chip_sum(c, (x - d) % NX, 0 if d > 0 else 256, 256)
            value = value + RR[c][pl.ds(RING["F", d][0], 256), :].astype(F32)
            RX[c][pl.ds(lo, size), :] = value.astype(BF)
            begin(ring_copy(c, ("L", d)))

    def ring_end(c):
        for half in (0, 1):
            now, old = (("L", 1), ("E", -1)) if half == 0 else (("L", -1), ("E", 1))
            value = chip_sum(c, x, half * 256, 256)
            for key in (old, now):
                ring_copy(c, key).wait_recv()
                value = value + RR[c][pl.ds(RING[key][0], 256), :].astype(F32)
            SO[half * 256:(half + 1) * 256, c * WIDE:(c + 1) * WIDE] = value

    def sum_slot(c, n):
        def run():
            xi, j = n % 16 // 4, n % 4
            if n < 16:
                sum_block(c, 2 * xi + other, j, XS[c], xi)
                if j == 3:
                    begin(swap_copy(c, xi))
            else:
                sum_block(c, 2 * xi + core, j, CS, xi)
        return run

    arrived = set()
    fillers = [edge_in.wait] + [transpose_slot(j) for j in range(CAP)]
    left = COUNT
    for is_send, c, key in PROGRAM:
        if is_send:
            gather_copy(c, key).start()
            continue
        if (c, key) not in arrived:
            arrived |= {(c, key), (c, TWIN[key])}
            pair_wait(c, ag_r, key)
        if c == 0:
            left -= 1
            if left == 0:
                fillers += [sum_slot(0, n) for n in range(32)]
                fillers += [None] * 2 + [lambda: ring_far(0)]
                fillers += [None] * 5 + [lambda: ring_near(0)]
        for _ in range(1 if left == 0 else 2):
            f = fillers.pop(0) if fillers else None
            if f is not None:
                f()
    for f in fillers:
        if f is not None:
            f()
    ring_end(0)

    for xi in range(NX):
        @pl.loop(0, 4)
        def _(j):
            sum_block(1, 2 * xi + other, j, XS[1], xi)

        begin(swap_copy(1, xi))

    @pl.loop(0, 4)
    def _(xi):
        for j in range(4):
            sum_block(1, 2 * xi + core, j, CS, xi)

    ring_far(1)
    ring_near(1)
    ring_end(1)

    T_DIM = (((1,), (1,)), ((), ()))
    C_DIM = (((0,), (0,)), ((), ()))

    @pl.loop(0, 4)
    def _(i):
        part = rows_of(i * BLK, BLK, BLK)
        s = SO[part, :]
        hi = s.astype(BF)
        lo = (s - hi.astype(F32)).astype(BF)
        SH[part, :] = hi
        mine = row * 4 + i
        pre = jnp.dot(hi, w_msg[...], preferred_element_type=F32)
        pre += jnp.dot(lo, w_msg[...], preferred_element_type=F32)
        pre += jnp.dot(F0[mine], w_self[:WIDE, :], preferred_element_type=F32)
        pre += jnp.dot(F1[mine], w_self[WIDE:, :], preferred_element_type=F32)
        pre += bias[...]
        real = mask[part, :]
        sig = jax.nn.sigmoid(pre)
        hidden[part, :] = (pre * sig * real).astype(BF)
        deriv = sig * (1.0 + pre * (1.0 - sig))
        gp = (gout[part, :].astype(F32) * real * deriv).astype(BF)
        GP[part, :] = gp
        h = lax.dot_general(gp, w_msg[...], T_DIM, preferred_element_type=F32).astype(BF)
        H0[col * 4 + i] = h[:, :WIDE]
        H1[col * 4 + i] = h[:, WIDE:]

    shares = {}
    SHARE = {
        ("X1", 1): (0, 1, False, -1, 0, 4), ("X1", -1): (1, -1, False, 1, 0, 4),
        ("X2", 1): (2, 1, False, -2, 0, 2), ("X2", -1): (3, -1, False, 2, 2, 2),
        ("S", 0): (4, 0, True, 0, 0, 4), ("S", -1): (5, 0, True, -1, 0, 4),
        ("S", 1): (6, 0, True, 1, 0, 4),
        ("S", 2): (7, 0, True, 2, 0, 2), ("S", 3): (8, 0, True, 2, 2, 2),
    }

    def share_copy(c, key):
        if (c, key) not in shares:
            i, dx, swap, origin, lo, size = SHARE[key]
            from_x = origin if swap else origin + dx
            block = (x + from_x) % NX * 2 + core
            part = H[c].at[pl.ds(block * 4 + lo, size)]
            i += 9 * c
            shares[c, key] = remote(part, part, h_s.at[i], h_r.at[i], col_device(dx, swap))
        return shares[c, key]

    def share_start(c):
        for key in (("X1", 1), ("X1", -1), ("S", 0)):
            begin(share_copy(c, key))

    def share_near(c):
        for d in (1, -1):
            share_copy(c, ("X1", d)).wait_recv()
            begin(share_copy(c, ("X2", d)))
            begin(share_copy(c, ("S", -d)))

    def share_far(c):
        for d in (1, -1):
            share_copy(c, ("X2", d)).wait_recv()
            begin(share_copy(c, ("S", 2 if d > 0 else 3)))

    def share_end(c):
        for n in (0, -1, 1, 2, 3):
            share_copy(c, ("S", n)).wait_recv()

    def term_slots(c, start, count, acc):
        def body(n, acc):
            for u in range(4):
                j = start + n * 4 + u
                h = H[c][tab[0, PROW + j]]
                at = AT[j]
                keep = tab[0, SAME + j].astype(F32)
                acc = acc * keep + jnp.dot(at, h, preferred_element_type=F32)
                U[c][j] = acc.astype(BF)
            return acc
        return lax.fori_loop(0, count // 4, body, acc)

    share_start(0)

    WG = WC

    @pl.loop(0, 1)
    def _(i):
        gp = GP[...]
        w1 = lax.dot_general(SH[...], gp, C_DIM, preferred_element_type=F32)
        for n in range(4):
            WG[n, 0:64, :] = w1[n * 64:(n + 1) * 64]
        for c in (0, 1):
            fc = F[c][pl.ds(row * 4, 4)].reshape(OWN, WIDE)
            w2 = lax.dot_general(fc, gp, C_DIM, preferred_element_type=F32)
            for n in range(2):
                WG[4 + 2 * c + n, 0:64, :] = w2[n * 64:(n + 1) * 64]
        b = jnp.sum(gp.astype(F32).reshape(64, 8, FEAT), axis=0)
        for n in range(8):
            WG[n, 64:72, :] = b
        GW[...] = lax.dot_general(gp, w_self[...], T_DIM, preferred_element_type=F32)

    share_near(0)
    share_start(1)
    share_far(0)
    share_end(0)
    zero = jnp.zeros((BLK, WIDE), F32)
    term_slots(0, 0, CAP, zero)

    stages = {}

    def stage_copy(kind, d):
        if (kind, d) not in stages:
            if kind == "col":
                to = (col + d) % NC
                stages[kind, d] = remote(
                    WC.at[to], WR.at[col], w_s.at[d], w_r.at[d], (row, to))
            elif kind == "z":
                to = (z + d) % NZ
                stages[kind, d] = remote(
                    ZS.at[to], ZR.at[z], w_s.at[8 + d], w_r.at[8 + d], plane_device(d, 0))
            elif kind == "y":
                stages[kind, d] = remote(
                    YR.at[y], YR.at[y], w_s.at[16 + d], w_r.at[16 + d], plane_device(0, d))
            elif kind == "zg":
                stages[kind, d] = remote(
                    ZG.at[z], ZG.at[z], w_s.at[20 + d], w_r.at[20 + d], plane_device(d, 0))
            else:
                to = (col + d) % NC
                stages[kind, d] = remote(
                    CG.at[col], CG.at[col], w_s.at[28 + d], w_r.at[28 + d], (row, to))
        return stages[kind, d]

    def stage_send(kind, n):
        for d in range(1, n):
            begin(stage_copy(kind, d))

    def stage_wait(kind, n):
        for d in range(1, n):
            stage_copy(kind, d).wait_recv()

    def weights_0():
        WR[col] = WC[col]
        stage_send("col", NC)

    def weights_1():
        stage_wait("col", NC)
        v = WR[0]
        for n in range(1, NC):
            v = v + WR[n]
        for n in range(NZ):
            ZS[n, 0:8, :] = v[n * 8:n * 8 + 8]
            ZS[n, 8:16, :] = v[64:72]
        ZR[z] = ZS[z]
        stage_send("z", NZ)

    def weights_2():
        stage_wait("z", NZ)
        v = ZR[0]
        for n in range(1, NZ):
            v = v + ZR[n]
        YR[y] = v
        stage_send("y", NY)

    def weights_3():
        stage_wait("y", NY)
        v = (YR[0] + YR[1]) + (YR[2] + YR[3])
        ZG[z] = v[0:8]
        bgrad[...] = jnp.sum(v[8:16], axis=0, keepdims=True) * FACTOR
        stage_send("zg", NZ)

    def weights_4():
        stage_wait("zg", NZ)
        for n in range(NZ):
            CG[col, n * 8:n * 8 + 8, :] = ZG[n]
        stage_send("cg", NC)

    def weights_5():
        stage_wait("cg", NC)
        for n in range(NC):
            wgrad[n * 64:(n + 1) * 64, :] = CG[n] * FACTOR

    reduces = {}

    def reduce_copy(c, key):
        if (c, key) not in reduces:
            axis, d = MESSAGES[key][:2]
            part = pl.ds(OFFSET[key], rows_in(MESSAGES[key]))
            target = plane_device(-d, 0) if axis == "z" else plane_device(0, -d)
            reduces[c, key] = remote(
                SS[c].at[part, :], SR[c].at[part, :], rs_s.at[c], rs_r.at[c, SLOT[key]], target)
        return reduces[c, key]

    def total_piece(c, block, n, lo, hi, children):
        value = U[c][tab[0, UIDX + block * 4 + n], lo:hi, :].astype(F32)
        for k in children:
            (b0, b1), rows = MESSAGES[k][4:6]
            if rows == (lo, hi) and b0 <= n < b1:
                at = OFFSET[k] + (n - b0) * (hi - lo)
                value = value + SR[c][pl.ds(at, hi - lo), :].astype(F32)
        return value

    waited = set()

    def reduce_wait(c, keys):
        for k in keys:
            if (c, k) not in waited:
                waited.add((c, k))
                waited.add((c, TWIN[k]))
                pair_wait(c, rs_r, k)

    def reduce_send(c, key):
        _, _, _, (dz, dy), (b0, b1), (lo, hi) = MESSAGES[key]
        children = CHILDREN[key]
        reduce_wait(c, children)
        block = (z + dz) % NZ * NY + (y + dy) % NY
        for n in range(b0, b1):
            at = OFFSET[key] + (n - b0) * (hi - lo)
            SS[c][pl.ds(at, hi - lo), :] = total_piece(c, block, n, lo, hi, children).astype(BF)
        reduce_copy(c, key).start()

    def finish(c):
        reduce_wait(c, ROOTS)
        part = slice(c * WIDE, (c + 1) * WIDE)
        for n in range(4):
            for lo, hi in ((0, CUT), (CUT, BLK)):
                a, b = n * BLK + lo, n * BLK + hi
                value = total_piece(c, row, n, lo, hi, ROOTS) * mask[a:b, :]
                gfeats[a:b, part] = (value + GW[a:b, part]).astype(BF)

    def edge_slot(s):
        def run():
            e = None
            for c in (0, 1):
                f = F[c][tab[0, FIDX + s]]
                d = lax.dot_general(H[c][s % TROWS], f, T_DIM, preferred_element_type=F32)
                e = d if e is None else e + d
            EB[s] = e.astype(BF)
        return run

    plan = [(1 - chunk, key) for chunk, key in reversed(ORDER)]
    later = next(i for i, (c, _) in enumerate(plan) if c == 1)

    def term_filler(n):
        def run():
            acc = zero if n == 0 else ACC[...]
            ACC[...] = term_slots(1, n * 8, 8, acc)
        return run

    def share_rest():
        share_far(1)
        share_end(1)

    edge_work = [lambda: share_near(1), weights_0] + [None] * 10 + [share_rest]
    edge_work += [term_filler(n) for n in range(CAP // 8)]
    pace = {later + 6: weights_1, later + 22: weights_2, later + 34: weights_3,
            later + 46: weights_4, later + 62: weights_5}
    for i, (c, key) in enumerate(plan):
        if i == later:
            for f in edge_work:
                if f is not None:
                    f()
            edge_work = [edge_slot(s) for s in range(CAP)]
        reduce_send(c, key)
        if i in pace:
            pace[i]()
        for _ in range(1 if i < later else 2):
            f = edge_work.pop(0) if edge_work else None
            if f is not None:
                f()
    for f in edge_work:
        f()
    edge_copy = pltpu.make_async_copy(EB, edge_out, loc.at[1])
    edge_copy.start()
    finish(0)
    finish(1)
    for copy in sent:
        copy.wait_send()
    for c in (0, 1):
        pltpu.make_async_copy(SS[c], SS[c], ag_s.at[c]).wait()
        pltpu.make_async_copy(SS[c], SS[c], rs_s.at[c]).wait()
    edge_copy.wait()


def run_kernel(tab, bias, mask, feats, w_msg, w_self, gout, edges):
    vm = pl.BlockSpec(memory_space=pltpu.VMEM)
    dma = pltpu.SemaphoreType.DMA
    b16 = lambda rows: pltpu.VMEM((rows, WIDE), BF)
    f32 = lambda *shape: pltpu.VMEM(shape, F32)
    blocks = lambda n: pltpu.VMEM((n, BLK, WIDE), BF)
    edge_shape = jax.ShapeDtypeStruct((CAP, BLK, BLK), BF)
    scratch = [
        blocks(TCOLS + 1), blocks(TCOLS + 1), blocks(CAP), blocks(CAP),
        blocks(CAP + 1), blocks(CAP + 1),
        b16(PLANE_ROWS), b16(PLANE_ROWS), b16(PLANE_ROWS), b16(PLANE_ROWS),
        blocks(TROWS), blocks(TROWS), blocks(CAP),
        b16(NX * OWN), b16(NX * OWN), b16(NX * OWN), b16(NX * OWN), f32(NX * OWN, WIDE),
        b16(1536), b16(1536), b16(1536), b16(1536),
        f32(OWN, FEAT), pltpu.VMEM((OWN, FEAT), BF), pltpu.VMEM((OWN, FEAT), BF), f32(OWN, FEAT),
        f32(NC, 72, FEAT), f32(NC, 72, FEAT), f32(NZ, 16, FEAT), f32(NZ, 16, FEAT),
        f32(NY, 16, FEAT), f32(NZ, 8, FEAT), f32(NC, 64, FEAT), f32(BLK, WIDE),
        dma((2,)), dma((2,)), dma((2, COUNT // 2)), dma((2,)), dma((2, COUNT // 2)),
        dma((20,)), dma((20,)), dma((18,)), dma((18,)), dma((36,)), dma((36,)),
    ]
    return pl.pallas_call(
        kernel,
        out_shape=(
            jax.ShapeDtypeStruct((OWN, FEAT), BF),
            jax.ShapeDtypeStruct((OWN, FEAT), BF),
            edge_shape,
            jax.ShapeDtypeStruct((2 * FEAT, FEAT), F32),
            jax.ShapeDtypeStruct((1, FEAT), F32),
        ),
        in_specs=[pl.BlockSpec(memory_space=pltpu.SMEM)] + [vm] * 6
        + [pl.BlockSpec(memory_space=pl.ANY)],
        out_specs=(vm, vm, pl.BlockSpec(memory_space=pl.ANY), vm, vm),
        scratch_shapes=scratch,
        compiler_params=pltpu.CompilerParams(
            collective_id=0, has_side_effects=True, vmem_limit_bytes=64 * 1024 * 1024 - 65536
        ),
    )(tab, bias, mask, feats, w_msg, w_self, gout, edges)


def hand_over(hidden, gfeats, edge, wgrad, bgrad):
    def body(h_in, g_in, e_in, w_in, b_in, h, g, e, w1, w2, b, sem):
        copies = [
            pltpu.make_async_copy(src, dst, sem.at[i]) for i, (src, dst) in enumerate((
                (e_in, e), (h_in, h), (g_in, g), (w_in.at[pl.ds(0, FEAT)], w1),
                (w_in.at[pl.ds(FEAT, FEAT)], w2), (b_in, b),
            ))
        ]
        for copy in copies:
            copy.start()
        for copy in copies:
            copy.wait()

    like = lambda shape, dtype: jax.ShapeDtypeStruct(shape, dtype)
    return pl.pallas_call(
        body,
        out_shape=(
            like((OWN, FEAT), BF), like((OWN, FEAT), BF), like((CAP, BLK, BLK), BF),
            like((FEAT, FEAT), F32), like((FEAT, FEAT), F32), like((1, FEAT), F32),
        ),
        in_specs=[pl.BlockSpec(memory_space=pltpu.VMEM)] * 5,
        out_specs=[pl.BlockSpec(memory_space=pl.ANY)] * 6,
        scratch_shapes=[pltpu.SemaphoreType.DMA((6,))],
    )(hidden, gfeats, edge, wgrad, bgrad)


def slot_tables(cols, count):
    s = jnp.arange(CAP, dtype=jnp.int32)
    key = jnp.where(s < count, cols, TCOLS)
    below = (key[None, :] < key[:, None]) | ((key[None, :] == key[:, None]) & (s[None, :] < s[:, None]))
    rank = jnp.sum(below.astype(jnp.int32), axis=1)
    place = (rank[None, :] == s[:, None]).astype(jnp.int32)
    perm = jnp.sum(place * s[None, :], axis=1)
    near = (key[None, :] == key[:, None]) & (s[None, :] < s[:, None])
    again = jnp.any(near, axis=1).astype(jnp.int32)
    same = jnp.sum(place * again[None, :], axis=1)
    m = jnp.arange(TCOLS, dtype=jnp.int32)
    last = jnp.sum((key[None, :] <= m[:, None]).astype(jnp.int32), axis=1) - 1
    has = jnp.any(key[None, :] == m[:, None], axis=1)
    uidx = jnp.where(has, last, CAP)
    return jnp.concatenate([key, perm, perm % TROWS, same, uidx])[None, :]


def per_device(feats, w_msg, w_self, bias, hit_mask, block_cols, block_count, edge_vals, grad_out):
    tab = slot_tables(block_cols[0, 0], block_count[0, 0])
    hidden, gfeats, edge, wgrad, bgrad = run_kernel(
        tab, bias[None, :], hit_mask.astype(F32)[:, None], feats, w_msg, w_self, grad_out,
        edge_vals.reshape(CAP, BLK, BLK),
    )
    hidden, gfeats, edge, g_msg, g_self, bgrad = hand_over(hidden, gfeats, edge, wgrad, bgrad)
    return (hidden, gfeats, edge.reshape(1, 1, CAP, BLK, BLK), g_msg, g_self, bgrad[0])


def solution(mesh):
    placed = (
        P(("row", "col"), None),
        P(),
        P(),
        P(),
        P(("row", "col")),
        P("row", "col", None),
        P("row", "col"),
        P("row", "col", None, None, None),
        P(("row", "col"), None),
    )
    return jax.shard_map(
        per_device,
        mesh=mesh,
        in_specs=placed,
        out_specs=(
            P(("row", "col"), None),
            P(("row", "col"), None),
            P("row", "col", None, None, None),
            P(),
            P(),
            P(),
        ),
        check_vma=False,
    )
```

```python
import heapq
import math

import jax
import jax.numpy as jnp
from jax import lax
from jax.experimental import pallas as pl
from jax.experimental.pallas import tpu as pltpu
from jax.sharding import PartitionSpec as P

NZ, NY, NX, NC = 8, 4, 4, 8
OWN, FEAT, WIDE, BLK = 512, 256, 128, 128
CAP, TROWS, TCOLS = 96, 32, 128
CUT = 48
HALF = {1: (0, 2), -1: (2, 4)}
ALL = (0, 4)
NEAR = CAP // 4 * 3
FIDX, PERM, PROW, SAME, UIDX = 0, 96, 192, 288, 384
MESH = pl.DeviceIdType.MESH
FACTOR = 1.0 / math.sqrt(OWN * NZ * NY * NC)
BF, F32 = jnp.bfloat16, jnp.float32


def plane_messages():
    out = {}
    low, high = (0, CUT), (CUT, BLK)
    for d in (1, -1):
        out["PY1", d] = ("y", d, (), (0, -d), ALL, low)
        out["QZ", d, 1] = ("z", d, (), (-d, 0), ALL, high)
    for d in (1, -1):
        out["PZ", d, 1, 0] = ("z", d, (), (-d, 0), ALL, low)
        out["QY1", d, 0] = ("y", d, (), (0, -d), ALL, high)
    for d in (1, -1):
        out["PY2", d] = ("y", d, (("PY1", d),), (0, -2 * d), HALF[d], low)
    first = {-1: (("PY1", 1),), 1: (("PY1", -1),), 2: (("PY2", 1), ("PY2", -1))}
    for o in (0, -1, 1, 2):
        for d in (1, -1):
            for t in (1, 2, 3, 4):
                if (o, t) == (0, 1):
                    continue
                parents = first[o] if t == 1 else (("PZ", d, t - 1, o),)
                out["PZ", d, t, o] = ("z", d, parents, (-t * d, o), HALF[d] if t == 4 else ALL, low)
    for d in (1, -1):
        for t in (2, 3, 4):
            blocks = HALF[d] if t == 4 else ALL
            out["QZ", d, t] = ("z", d, (("QZ", d, t - 1),), (-t * d, 0), blocks, high)
    for oz in (0, -1, 1, -2, 2, -3, 3, 4):
        for d in (1, -1):
            if oz == 4:
                parents = (("QZ", 1, 4), ("QZ", -1, 4))
            else:
                parents = (("QZ", 1 if oz < 0 else -1, abs(oz)),)
            if oz:
                out["QY1", d, oz] = ("y", d, parents, (oz, -d), ALL, high)
            out["QY2", d, oz] = ("y", d, (("QY1", d, oz),), (oz, -2 * d), HALF[d], high)
    return out


def rows_in(message):
    (b0, b1), (lo, hi) = message[4:6]
    return (b1 - b0) * (hi - lo)


RATE, HOP, AHEAD = 46e3, 1.7, 1.5


class Model:
    def __init__(self, messages, back):
        self.messages, self.back = messages, back
        self.took = {key: rows_in(m) * WIDE * 2 / RATE for key, m in messages.items()}
        self.after = {key: [k for k, m in messages.items() if key in m[2]] for key in messages}
        self.links = {m[:2]: 0.0 for m in messages.values()}
        self.landed, self.got, self.flying, self.program = set(), set(), [], []
        self.now, self.weight = 0.0, {}
        self.open, self.waiting = set(), {(c, key) for c in (0, 1) for key in messages}

    def needs(self, key):
        if self.back:
            return self.after[key]
        return self.messages[key][2]

    def path(self, key):
        if key not in self.weight:
            nexts = self.messages[key][2] if self.back else self.after[key]
            self.weight[key] = self.took[key] + HOP + max([self.path(k) for k in nexts] + [0.0])
        return self.weight[key]

    def land(self):
        while self.flying and self.flying[0][0] <= self.now + 1e-9:
            _, _, c, key = heapq.heappop(self.flying)
            self.landed.add((c, key))
            twin = (c, (key[0], -key[1]) + key[2:])
            if twin in self.landed:
                self.got |= {(c, key), twin}
                if not self.back:
                    self.program.append(("recv", c, key))
                    self.now += 0.03

    def send(self):
        best = None
        for c, key in self.waiting:
            link = self.messages[key][:2]
            if c in self.open and self.links[link] - AHEAD <= self.now + 1e-9:
                if all((c, k) in self.got for k in self.needs(key)):
                    rank = (c, -self.path(key), NUMBER[key])
                    if best is None or rank < best[0]:
                        best = (rank, c, key, link)
        if best is None:
            return False
        _, c, key, link = best
        self.waiting.remove((c, key))
        if self.back:
            self.now += 0.05 + self.took[key] * 0.08
        self.links[link] = max(self.now, self.links[link]) + self.took[key]
        heapq.heappush(self.flying, (self.links[link] + HOP, len(self.program), c, key))
        self.program.append(("send", c, key))
        return True

    def run(self, timed, spare):
        last, timed, spare = 0.0, list(timed(self)), list(spare(self))
        while True:
            self.land()
            if self.send():
                continue
            times = [f[0] for f in self.flying[:1]]
            times += [self.links[self.messages[k][:2]] - AHEAD for c, k in self.waiting
                      if c in self.open and all((c, n) in self.got for n in self.needs(k))]
            soon = min([t for t in times if t > self.now] + [1e9])
            if timed and timed[0][3](self) and last + timed[0][2] <= self.now + 1e-9:
                name, cost = timed.pop(0)[:2]
            elif spare and spare[0][2](self) and soon - self.now >= 0.5 * spare[0][1]:
                name, cost = spare.pop(0)[:2]
            else:
                if timed and timed[0][3](self):
                    soon = min(soon, max(last + timed[0][2], self.now + 1e-6))
                if soon > 1e8:
                    return self.program
                self.now = soon
                continue
            self.program.append(("fill",) + name)
            self.now += cost
            if not spare or name[0] not in ("turn", "edge"):
                last = self.now
            if name == ("gate",):
                self.open.add(1)


def gather_program(messages):
    model = Model(messages, False)
    model.open = {0, 1}
    full = lambda m: sum(1 for c, _ in m.got if c == 0) == len(messages)
    timed = [(("sum", n), 0.12, 0.0, full) for n in range(32)]
    timed += [(("far",), 0.2, 1.0, full), (("early",), 0.2, 0.0, full),
              (("near",), 0.2, 3.0, full), (("end",), 0.2, 4.0, full)]
    started = lambda m: m.now > 3.0
    spare = [(("turn", n), 0.12, started) for n in range(CAP + 1)]
    return model.run(lambda m: timed, lambda m: spare), model.now


def reduce_program(messages):
    model = Model(messages, True)
    model.open = {0}
    always = lambda m: True
    timed = [(("share_near",), 0.1, 1.0, always), (("weights", 0), 0.5, 0.0, always),
             (("share_far",), 0.1, 3.5, always), (("share_end",), 0.1, 1.5, always)]
    timed += [(("term", n), 0.4, 0.0, always) for n in range(CAP // 8)] + [(("gate",), 0.0, 0.0, always)]
    timed += [(("weights", n), 0.3, 0.0 if n == 1 else 3.5, always) for n in range(1, 6)]
    opened = lambda m: 1 in m.open
    spare = [(("edge", n), 0.1, opened) for n in range(CAP)]
    return model.run(lambda m: timed, lambda m: spare), model.now


MESSAGES = plane_messages()
NUMBER = {key: i for i, key in enumerate(MESSAGES)}
GATHER, SPAN = gather_program(MESSAGES)
REDUCE, BACK = reduce_program(MESSAGES)
TWIN = {key: (key[0], -key[1]) + key[2:] for key in MESSAGES}
PAIR = {key: NUMBER[key if key[1] > 0 else TWIN[key]] for key in MESSAGES}
COUNT = len(MESSAGES)
OFFSET = {}
_total = 0
for _key, _m in MESSAGES.items():
    OFFSET[_key] = _total
    _total += rows_in(_m)
PLANE_ROWS = _total
SLOT = {key: sorted(set(PAIR.values())).index(PAIR[key]) for key in MESSAGES}
CHILDREN = {key: [k for k, m in MESSAGES.items() if key in m[2]] for key in MESSAGES}
ROOTS = [k for k, m in MESSAGES.items() if not m[2]]


def kernel(
    tab, bias_in, mask_in, feats_in, w_msg_in, w_self_in, gout_in, edges,
    hidden, gfeats, EB, wgrad, bgrad,
    bias, mask, feats, w_msg, w_self, gout, HF0, HF1,
    F0, F1, A, AT, U0, U1, SS0, SS1, SR0, SR1, H0, H1,
    XS0, XS1, XR0, XR1, CS, RX0, RX1, RR0, RR1, SO, SH, GP, GW,
    WC, WR, ZS, ZR, YR, ZG, CG, ACC, MASK,
    loc, ag_s, ag_r, rs_s, rs_r, x_s, x_r, h_s, h_r, w_s, w_r,
):
    F, U, SS, SR, H = (F0, F1), (U0, U1), (SS0, SS1), (SR0, SR1), (H0, H1)
    HF = (HF0, HF1)
    XS, XR, RX, RR = (XS0, XS1), (XR0, XR1), (RX0, RX1), (RR0, RR1)
    row = lax.axis_index("row")
    col = lax.axis_index("col")
    z, y = row // NY, row % NY
    x, core = col // 2, col % 2
    other = 1 - core

    def plane_device(dz, dy):
        return ((z + dz) % NZ * NY + (y + dy) % NY, col)

    def col_device(dx, swap=False):
        return (row, (x + dx) % NX * 2 + (other if swap else core))

    def remote(src, dst, ssem, rsem, device):
        return pltpu.make_async_remote_copy(
            src_ref=src, dst_ref=dst, send_sem=ssem, recv_sem=rsem,
            device_id=device, device_id_type=MESH,
        )

    def rows_of(start, size, step=16):
        return pl.ds(pl.multiple_of(start, step), size)

    edge_in = pltpu.make_async_copy(edges, A, loc.at[0])
    loads = [
        pltpu.make_async_copy(src, dst, loc.at[i + 1])
        for i, (src, dst) in enumerate((
            (feats_in, feats), (mask_in, mask), (w_msg_in, w_msg), (w_self_in, w_self),
            (gout_in, gout), (bias_in, bias),
        ))
    ]
    for load in loads[:2]:
        load.start()
    edge_in.start()
    for load in loads[2:]:
        load.start()
    for load in loads[:2]:
        load.wait()
    flags = mask[...].astype(F32)
    for n in range(4):
        real = jnp.broadcast_to(flags[n:n + 1, :], (BLK, BLK)).T
        MASK[n * BLK:(n + 1) * BLK, :] = real
        for c in (0, 1):
            f = feats[n * BLK:(n + 1) * BLK, c * WIDE:(c + 1) * WIDE]
            F[c][row * 4 + n] = f * real.astype(BF)
    for c in (0, 1):
        F[c][TCOLS] = jnp.zeros((BLK, WIDE), BF)
        U[c][CAP] = jnp.zeros((BLK, WIDE), BF)

    barrier = pltpu.get_barrier_semaphore()
    peers = [plane_device(0, 1), plane_device(0, -1), plane_device(1, 0), plane_device(-1, 0)]
    peers += [col_device(1), col_device(-1), col_device(0, True)]
    for peer in peers:
        pl.semaphore_signal(barrier, inc=1, device_id=peer, device_id_type=MESH)
    pl.semaphore_wait(barrier, len(peers))

    gathers = {}

    def gather_copy(c, key):
        if (c, key) not in gathers:
            axis, d, _, (dz, dy), (b0, b1), (lo, hi) = MESSAGES[key]
            sz, sy = (dz + d, dy) if axis == "z" else (dz, dy + d)
            block = (z + sz) % NZ * NY + (y + sy) % NY
            part = F[c].at[pl.ds(block * 4 + b0, b1 - b0), pl.ds(lo, hi - lo), :]
            target = plane_device(d, 0) if axis == "z" else plane_device(0, d)
            gathers[c, key] = remote(part, part, ag_s.at[c], ag_r.at[c, SLOT[key]], target)
        return gathers[c, key]

    def pair_wait(c, sem, key):
        part = SR[c].at[pl.ds(0, 2 * rows_in(MESSAGES[key])), :]
        pltpu.make_async_copy(part, part, sem.at[c, SLOT[key]]).wait()

    def transpose_slot(j):
        def run():
            AT[j] = A[tab[0, PERM + j]].astype(F32).T.astype(BF)
        return run

    def sum_block(c, owner, j, dest, place):
        l = owner * 4 + j
        acc = None
        for k in range(3):
            s = k * TROWS + l
            d = jnp.dot(A[s], F[c][tab[0, FIDX + s]], preferred_element_type=F32)
            acc = d if acc is None else acc + d
        dest[rows_of(place * OWN + j * BLK, BLK, BLK), :] = acc.astype(dest.dtype)

    swaps = {}

    def swap_copy(c, rel):
        if (c, rel) not in swaps:
            part = rows_of((x + rel) % NX * OWN, OWN)
            swaps[c, rel] = remote(
                XS[c].at[part, :], XR[c].at[part, :], x_s.at[c], x_r.at[c * 10 + rel],
                col_device(0, True),
            )
        return swaps[c, rel]

    rings = {}
    RING = {
        ("F", 1): (0, 256), ("F", -1): (256, 256), ("E", 1): (512, 256), ("E", -1): (768, 256),
        ("L", 1): (1024, 256), ("L", -1): (1280, 256),
    }

    def ring_copy(c, key):
        if (c, key) not in rings:
            lo, size = RING[key]
            i = c * 10 + 4 + list(RING).index(key)
            rings[c, key] = remote(
                RX[c].at[pl.ds(lo, size), :], RR[c].at[pl.ds(lo, size), :],
                x_s.at[2 + c], x_r.at[i], col_device(-key[1]),
            )
        return rings[c, key]

    def chip_sum(c, xi, lo, size):
        part = rows_of(xi * OWN + lo, size)
        return CS[part, :] + XR[c][part, :].astype(F32)

    def ring_far(c):
        swap_copy(c, 2).wait_recv()
        for d in (1, -1):
            lo, size = RING["F", d]
            RX[c][pl.ds(lo, size), :] = chip_sum(
                c, (x + 2) % NX, 0 if d > 0 else 256, 256).astype(BF)
            ring_copy(c, ("F", d)).start()

    def ring_early(c):
        for d in (1, -1):
            swap_copy(c, 3 if d > 0 else 1).wait_recv()
            lo, size = RING["E", d]
            RX[c][pl.ds(lo, size), :] = chip_sum(
                c, (x - d) % NX, 256 if d > 0 else 0, 256).astype(BF)
            ring_copy(c, ("E", d)).start()

    def ring_near(c):
        for d in (1, -1):
            ring_copy(c, ("F", d)).wait_recv()
            lo, size = RING["L", d]
            value = chip_sum(c, (x - d) % NX, 0 if d > 0 else 256, 256)
            value = value + RR[c][pl.ds(RING["F", d][0], 256), :].astype(F32)
            RX[c][pl.ds(lo, size), :] = value.astype(BF)
            ring_copy(c, ("L", d)).start()

    def ring_end(c):
        swap_copy(c, 0).wait_recv()
        for half in (0, 1):
            now, old = (("L", 1), ("E", -1)) if half == 0 else (("L", -1), ("E", 1))
            value = chip_sum(c, x, half * 256, 256)
            for key in (old, now):
                ring_copy(c, key).wait_recv()
                value = value + RR[c][pl.ds(RING[key][0], 256), :].astype(F32)
            SO[half * 256:(half + 1) * 256, c * WIDE:(c + 1) * WIDE] = value

    TURN = (2, 1, 3, 0)

    def sum_slot(c, n):
        rel, j = TURN[n % 16 // 4], n % 4
        xi = (x + rel) % NX
        if n < 16:
            sum_block(c, 2 * xi + other, j, XS[c], xi)
            if j == 3:
                swap_copy(c, rel).start()
        else:
            sum_block(c, 2 * xi + core, j, CS, xi)

    def sum_group(c, rel, mine):
        xi = (x + rel) % NX

        for j in range(4):
            if mine:
                sum_block(c, 2 * xi + core, j, CS, xi)
            else:
                sum_block(c, 2 * xi + other, j, XS[c], xi)

    def turn(n):
        if n == 0:
            edge_in.wait()
            for load in loads[2:]:
                load.wait()
        else:
            transpose_slot(n - 1)()

    gather_steps = {
        "turn": turn, "sum": lambda n: sum_slot(0, n), "far": lambda: ring_far(0),
        "early": lambda: ring_early(0), "near": lambda: ring_near(0), "end": lambda: ring_end(0),
    }
    for step, *what in GATHER:
        if step == "send":
            gather_copy(*what).start()
        elif step == "recv":
            pair_wait(what[0], ag_r, what[1])
        else:
            gather_steps[what[0]](*what[1:])

    for rel in TURN:
        sum_group(1, rel, False)
        swap_copy(1, rel).start()
    sum_group(1, 2, True)
    ring_far(1)
    sum_group(1, 1, True)
    sum_group(1, 3, True)
    ring_early(1)
    sum_group(1, 0, True)
    ring_near(1)
    ring_end(1)

    T_DIM = (((1,), (1,)), ((), ()))
    C_DIM = (((0,), (0,)), ((), ()))

    @pl.loop(0, 4)
    def _(i):
        part = rows_of(i * BLK, BLK, BLK)
        s = SO[part, :]
        hi = s.astype(BF)
        lo = (s - hi.astype(F32)).astype(BF)
        SH[part, :] = hi
        mine = row * 4 + i
        pre = jnp.dot(hi, w_msg[...], preferred_element_type=F32)
        pre += jnp.dot(lo, w_msg[...], preferred_element_type=F32)
        pre += jnp.dot(F0[mine], w_self[:WIDE, :], preferred_element_type=F32)
        pre += jnp.dot(F1[mine], w_self[WIDE:, :], preferred_element_type=F32)
        pre += bias[...]
        real = jnp.concatenate([MASK[part, :], MASK[part, :]], axis=1)
        sig = jax.nn.sigmoid(pre)
        hidden[part, :] = (pre * sig * real).astype(BF)
        deriv = sig * (1.0 + pre * (1.0 - sig))
        gp = (gout[part, :].astype(F32) * real * deriv).astype(BF)
        GP[part, :] = gp
        h = lax.dot_general(gp, w_msg[...], T_DIM, preferred_element_type=F32).astype(BF)
        H0[col * 4 + i] = h[:, :WIDE]
        H1[col * 4 + i] = h[:, WIDE:]

    shares = {}
    SHARE = {
        ("X1", 1): (0, 1, False, -1, 0, 4), ("X1", -1): (1, -1, False, 1, 0, 4),
        ("X2", 1): (2, 1, False, -2, 0, 2), ("X2", -1): (3, -1, False, 2, 2, 2),
        ("S", 0): (4, 0, True, 0, 0, 4), ("S", -1): (5, 0, True, -1, 0, 4),
        ("S", 1): (6, 0, True, 1, 0, 4),
        ("S", 2): (7, 0, True, 2, 0, 2), ("S", 3): (8, 0, True, 2, 2, 2),
    }

    def share_copy(c, key):
        if (c, key) not in shares:
            i, dx, swap, origin, lo, size = SHARE[key]
            from_x = origin if swap else origin + dx
            block = (x + from_x) % NX * 2 + core
            part = H[c].at[pl.ds(block * 4 + lo, size)]
            land = part
            if key[0] == "X2" or lo + size != 4 or key[1] == 3:
                land = HF[c].at[pl.ds(core * 4 + lo, size)]
            if key[0] == "S" and key[1] in (2, 3):
                part = land
            i += 9 * c
            shares[c, key] = remote(part, land, h_s.at[c], h_r.at[i], col_device(dx, swap))
        return shares[c, key]

    def share_start(c):
        for key in (("X1", 1), ("X1", -1), ("S", 0)):
            share_copy(c, key).start()

    def share_near(c):
        for d in (1, -1):
            share_copy(c, ("X1", d)).wait_recv()
            share_copy(c, ("X2", d)).start()
            share_copy(c, ("S", -d)).start()

    def share_far(c):
        for d in (1, -1):
            share_copy(c, ("X2", d)).wait_recv()
            share_copy(c, ("S", 2 if d > 0 else 3)).start()

    def share_end(c, which):
        for n in which:
            share_copy(c, ("S", n)).wait_recv()
        if 3 in which:
            for n in range(8):
                H[c][(x + 2) % NX * 8 + n] = HF[c][n]

    def term_slots(c, start, count, acc, late=False):
        def body(n, acc):
            for u in range(4):
                j = start + n * 4 + u
                h = HF[c][tab[0, PROW + j] & 7] if late else H[c][tab[0, PROW + j]]
                at = AT[j]
                keep = tab[0, SAME + j].astype(F32)
                acc = acc * keep + jnp.dot(at, h, preferred_element_type=F32)
                U[c][j] = acc.astype(BF)
            return acc
        return lax.fori_loop(0, count // 4, body, acc)

    share_start(0)

    WG = WC

    @pl.loop(0, 1)
    def _(i):
        gp = GP[...]
        w1 = lax.dot_general(SH[...], gp, C_DIM, preferred_element_type=F32)
        for n in range(4):
            WG[n, 0:64, :] = w1[n * 64:(n + 1) * 64]
        for c in (0, 1):
            fc = F[c][pl.ds(row * 4, 4)].reshape(OWN, WIDE)
            w2 = lax.dot_general(fc, gp, C_DIM, preferred_element_type=F32)
            for n in range(2):
                WG[4 + 2 * c + n, 0:64, :] = w2[n * 64:(n + 1) * 64]
        b = jnp.sum(gp.astype(F32).reshape(64, 8, FEAT), axis=0)
        for n in range(8):
            WG[n, 64:72, :] = b
        GW[...] = lax.dot_general(gp, w_self[...], T_DIM, preferred_element_type=F32)

    share_near(0)
    share_start(1)
    share_end(0, (0, -1, 1))
    zero = jnp.zeros((BLK, WIDE), F32)
    acc = term_slots(0, 0, 32, zero)
    share_far(0)
    term_slots(0, 32, NEAR - 32, acc)
    share_end(0, (2, 3))
    term_slots(0, NEAR, CAP - NEAR, zero, late=True)

    STAGES = {"col": (0, NC, WR), "z": (1, NZ, ZR), "y": (2, NY, YR), "zg": (3, NZ, ZG), "cg": (4, NC, CG)}

    def stage_send(kind):
        i, n, _ = STAGES[kind]
        for d in range(1, n):
            to_col, to_z = (col + d) % NC, (z + d) % NZ
            src, dst, device = {
                "col": (WC.at[to_col], WR.at[col], (row, to_col)),
                "z": (ZS.at[to_z], ZR.at[z], plane_device(d, 0)),
                "y": (YR.at[y], YR.at[y], plane_device(0, d)),
                "zg": (ZG.at[z], ZG.at[z], plane_device(d, 0)),
                "cg": (CG.at[col], CG.at[col], (row, to_col)),
            }[kind]
            remote(src, dst, w_s.at[i], w_r.at[i], device).start()

    def stage_wait(kind, sems=None):
        i, n, buf = STAGES[kind]
        part = buf.at[pl.ds(0, n - 1)]
        pltpu.make_async_copy(part, part, (w_r if sems is None else sems).at[i]).wait()

    def weights_0():
        WR[col] = WC[col]
        stage_send("col")

    def weights_1():
        stage_wait("col")
        v = WR[0]
        for n in range(1, NC):
            v = v + WR[n]
        for n in range(NZ):
            ZS[n] = jnp.concatenate([v[n * 8:n * 8 + 8], v[64:72]], axis=0).astype(BF)
        ZR[z] = ZS[z]
        stage_send("z")

    def weights_2():
        stage_wait("z")
        v = ZR[0].astype(F32)
        for n in range(1, NZ):
            v = v + ZR[n].astype(F32)
        YR[y] = v.astype(BF)
        stage_send("y")

    def weights_3():
        stage_wait("y")
        v = YR[0].astype(F32)
        for n in range(1, NY):
            v = v + YR[n].astype(F32)
        ZG[z] = v[0:8].astype(BF)
        bgrad[...] = jnp.sum(v[8:16], axis=0, keepdims=True) * FACTOR
        stage_send("zg")

    def weights_4():
        stage_wait("zg")
        for n in range(NZ):
            CG[col, n * 8:n * 8 + 8, :] = ZG[n]
        stage_send("cg")

    def weights_5():
        stage_wait("cg")
        for n in range(NC):
            wgrad[n * 64:(n + 1) * 64, :] = CG[n].astype(F32) * FACTOR

    reduces = {}

    def reduce_copy(c, key):
        if (c, key) not in reduces:
            axis, d = MESSAGES[key][:2]
            part = pl.ds(OFFSET[key], rows_in(MESSAGES[key]))
            target = plane_device(-d, 0) if axis == "z" else plane_device(0, -d)
            reduces[c, key] = remote(
                SS[c].at[part, :], SR[c].at[part, :], rs_s.at[c], rs_r.at[c, SLOT[key]], target)
        return reduces[c, key]

    def total_piece(c, block, n, lo, hi, children):
        m = UIDX + block * 4 + n
        value = U[c][tab[0, m], lo:hi, :].astype(F32) + U[c][tab[0, m + TCOLS], lo:hi, :].astype(F32)
        for k in children:
            (b0, b1), rows = MESSAGES[k][4:6]
            if rows == (lo, hi) and b0 <= n < b1:
                at = OFFSET[k] + (n - b0) * (hi - lo)
                value = value + SR[c][pl.ds(at, hi - lo), :].astype(F32)
        return value

    waited = set()

    def reduce_wait(c, keys):
        for k in keys:
            if (c, k) not in waited:
                waited.add((c, k))
                waited.add((c, TWIN[k]))
                pair_wait(c, rs_r, k)

    def reduce_send(c, key):
        _, _, _, (dz, dy), (b0, b1), (lo, hi) = MESSAGES[key]
        children = CHILDREN[key]
        reduce_wait(c, children)
        block = (z + dz) % NZ * NY + (y + dy) % NY
        for n in range(b0, b1):
            at = OFFSET[key] + (n - b0) * (hi - lo)
            SS[c][pl.ds(at, hi - lo), :] = total_piece(c, block, n, lo, hi, children).astype(BF)
        reduce_copy(c, key).start()

    def finish(c):
        reduce_wait(c, ROOTS)
        part = slice(c * WIDE, (c + 1) * WIDE)
        for n in range(4):
            for lo, hi in ((0, CUT), (CUT, BLK)):
                a, b = n * BLK + lo, n * BLK + hi
                value = total_piece(c, row, n, lo, hi, ROOTS) * MASK[a:b, :]
                gfeats[a:b, part] = (value + GW[a:b, part]).astype(BF)

    def edge_slot(s):
        def run():
            e = None
            for c in (0, 1):
                f = F[c][tab[0, FIDX + s]]
                d = lax.dot_general(H[c][s % TROWS], f, T_DIM, preferred_element_type=F32)
                e = d if e is None else e + d
            EB[s] = e.astype(BF)
        return run

    def term_filler(n):
        acc = zero if n * 8 in (0, NEAR) else ACC[...]
        ACC[...] = term_slots(1, n * 8, 8, acc)

    weights = (weights_0, weights_1, weights_2, weights_3, weights_4, weights_5)
    reduce_steps = {
        "share_near": lambda: share_near(1), "share_far": lambda: share_far(1),
        "share_end": lambda: share_end(1, (0, -1, 1, 2, 3)), "gate": lambda: None,
        "weights": lambda n: weights[n](), "term": term_filler, "edge": lambda n: edge_slot(n)(),
    }
    for step, *what in REDUCE:
        if step == "send":
            reduce_send(*what)
        else:
            reduce_steps[what[0]](*what[1:])
    finish(0)
    finish(1)
    for kind in STAGES:
        stage_wait(kind, w_s)
    for c in (0, 1):
        near = H[c].at[pl.ds(0, 28)]
        pltpu.make_async_copy(near, near, h_s.at[c]).wait()
        pltpu.make_async_copy(XS[c], XS[c], x_s.at[c]).wait()
        pltpu.make_async_copy(RX[c], RX[c], x_s.at[2 + c]).wait()
        pltpu.make_async_copy(SS[c], SS[c], ag_s.at[c]).wait()
        pltpu.make_async_copy(SS[c], SS[c], rs_s.at[c]).wait()


def run_kernel(tab, bias, mask, feats, w_msg, w_self, gout, edges):
    vm = pl.BlockSpec(memory_space=pltpu.VMEM)
    dma = pltpu.SemaphoreType.DMA
    b16 = lambda rows: pltpu.VMEM((rows, WIDE), BF)
    f32 = lambda *shape: pltpu.VMEM(shape, F32)
    half = lambda *shape: pltpu.VMEM(shape, BF)
    blocks = lambda n: pltpu.VMEM((n, BLK, WIDE), BF)
    edge_shape = jax.ShapeDtypeStruct((CAP, BLK, BLK), BF)
    scratch = [
        f32(1, FEAT), pltpu.VMEM((4, BLK), jnp.int32), pltpu.VMEM((OWN, FEAT), BF),
        pltpu.VMEM((FEAT, FEAT), BF), pltpu.VMEM((FEAT, FEAT), BF), pltpu.VMEM((OWN, FEAT), BF),
        pltpu.VMEM((8, BLK, WIDE), BF), pltpu.VMEM((8, BLK, WIDE), BF),
        blocks(TCOLS + 1), blocks(TCOLS + 1), blocks(CAP), blocks(CAP),
        blocks(CAP + 1), blocks(CAP + 1),
        b16(PLANE_ROWS), b16(PLANE_ROWS), b16(PLANE_ROWS), b16(PLANE_ROWS),
        blocks(TROWS), blocks(TROWS),
        b16(NX * OWN), b16(NX * OWN), b16(NX * OWN), b16(NX * OWN), f32(NX * OWN, WIDE),
        b16(1536), b16(1536), b16(1536), b16(1536),
        f32(OWN, FEAT), pltpu.VMEM((OWN, FEAT), BF), pltpu.VMEM((OWN, FEAT), BF), f32(OWN, FEAT),
        f32(NC, 72, FEAT), f32(NC, 72, FEAT), half(NZ, 16, FEAT), half(NZ, 16, FEAT),
        half(NY, 16, FEAT), half(NZ, 8, FEAT), half(NC, 64, FEAT), f32(BLK, WIDE), f32(OWN, WIDE),
        dma((7,)), dma((2,)), dma((2, COUNT // 2)), dma((2,)), dma((2, COUNT // 2)),
        dma((4,)), dma((20,)), dma((2,)), dma((18,)), dma((5,)), dma((5,)),
    ]
    return pl.pallas_call(
        kernel,
        out_shape=(
            jax.ShapeDtypeStruct((OWN, FEAT), BF),
            jax.ShapeDtypeStruct((OWN, FEAT), BF),
            edge_shape,
            jax.ShapeDtypeStruct((2 * FEAT, FEAT), F32),
            jax.ShapeDtypeStruct((1, FEAT), F32),
        ),
        in_specs=[pl.BlockSpec(memory_space=pltpu.SMEM)]
        + [pl.BlockSpec(memory_space=pltpu.HBM)] * 7,
        out_specs=(vm,) * 5,
        scratch_shapes=scratch,
        compiler_params=pltpu.CompilerParams(
            collective_id=0, has_side_effects=True, vmem_limit_bytes=48 * 1024 * 1024
        ),
    )(tab, *[pltpu.with_memory_space_constraint(v, pltpu.HBM)
             for v in (bias, mask, feats, w_msg, w_self, gout, edges)])


def hand_over(hidden, gfeats, edge, wgrad, bgrad):
    def body(h_in, g_in, e_in, w_in, b_in, h, g, e, w1, w2, b, sem):
        copies = [
            pltpu.make_async_copy(src, dst, sem.at[i]) for i, (src, dst) in enumerate((
                (e_in, e), (h_in, h), (g_in, g), (w_in.at[pl.ds(0, FEAT)], w1),
                (w_in.at[pl.ds(FEAT, FEAT)], w2), (b_in, b),
            ))
        ]
        for copy in copies:
            copy.start()
        for copy in copies:
            copy.wait()

    like = lambda shape, dtype: jax.ShapeDtypeStruct(shape, dtype)
    return pl.pallas_call(
        body,
        out_shape=(
            like((OWN, FEAT), BF), like((OWN, FEAT), BF), like((CAP, BLK, BLK), BF),
            like((FEAT, FEAT), F32), like((FEAT, FEAT), F32), like((1, FEAT), F32),
        ),
        in_specs=[pl.BlockSpec(memory_space=pltpu.VMEM)] * 5,
        out_specs=[pl.BlockSpec(memory_space=pl.ANY)] * 6,
        scratch_shapes=[pltpu.SemaphoreType.DMA((6,))],
        compiler_params=pltpu.CompilerParams(vmem_limit_bytes=8 * 1024 * 1024),
    )(hidden, gfeats, edge, wgrad, bgrad)


def slot_tables(cols, count, far):
    s = jnp.arange(CAP, dtype=jnp.int32)
    key = jnp.where(s < count, cols, TCOLS)
    late = s % TROWS // 8 == far
    order = key + jnp.where(late, TCOLS + 1, 0)
    before = (order[None, :] == order[:, None]) & (s[None, :] < s[:, None])
    rank = jnp.sum(((order[None, :] < order[:, None]) | before).astype(jnp.int32), axis=1)
    again = jnp.any(before, axis=1).astype(jnp.int32)
    place = (rank[None, :] == s[:, None]).astype(jnp.int32)
    perm = jnp.sum(place * s[None, :], axis=1)
    same = jnp.sum(place * again[None, :], axis=1)
    m = jnp.arange(2 * TCOLS, dtype=jnp.int32)
    want = m + jnp.where(m < TCOLS, 0, 1)
    last = jnp.max(jnp.where(order[None, :] == want[:, None], rank[None, :], -1), axis=1)
    uidx = jnp.where(last < 0, CAP, last)
    return jnp.concatenate([key, perm, perm % TROWS, same, uidx])[None, :]


def per_device(feats, w_msg, w_self, bias, hit_mask, block_cols, block_count, edge_vals, grad_out):
    far = (lax.axis_index("col") // 2 + 2) % NX
    tab = slot_tables(block_cols[0, 0], block_count[0, 0], far)
    hidden, gfeats, edge, wgrad, bgrad = run_kernel(
        tab, bias[None, :], hit_mask.reshape(4, BLK), feats, w_msg, w_self, grad_out,
        edge_vals.reshape(CAP, BLK, BLK),
    )
    hidden, gfeats, edge, g_msg, g_self, bgrad = hand_over(hidden, gfeats, edge, wgrad, bgrad)
    return (hidden, gfeats, edge.reshape(1, 1, CAP, BLK, BLK), g_msg, g_self, bgrad[0])


def solution(mesh):
    placed = (
        P(("row", "col"), None),
        P(),
        P(),
        P(),
        P(("row", "col")),
        P("row", "col", None),
        P("row", "col"),
        P("row", "col", None, None, None),
        P(("row", "col"), None),
    )
    return jax.shard_map(
        per_device,
        mesh=mesh,
        in_specs=placed,
        out_specs=(
            P(("row", "col"), None),
            P(("row", "col"), None),
            P("row", "col", None, None, None),
            P(),
            P(),
            P(),
        ),
        check_vma=False,
    )
```

```python
import heapq
import math

import jax
import jax.numpy as jnp
from jax import lax
from jax.experimental import pallas as pl
from jax.experimental.pallas import tpu as pltpu
from jax.sharding import PartitionSpec as P

NZ, NY, NX, NC = 8, 4, 4, 8
OWN, FEAT, WIDE, BLK = 512, 256, 128, 128
CAP, TROWS, TCOLS = 96, 32, 128
CUT = 48
HALF = {1: (0, 2), -1: (2, 4)}
ALL = (0, 4)
NEAR = CAP // 4 * 3
FIDX, PERM, PROW, SAME, UIDX = 0, 96, 192, 288, 384
MESH = pl.DeviceIdType.MESH
FACTOR = 1.0 / math.sqrt(OWN * NZ * NY * NC)
BF, F32 = jnp.bfloat16, jnp.float32


def plane_messages():
    out = {}
    low, high = (0, CUT), (CUT, BLK)
    for d in (1, -1):
        out["PY1", d] = ("y", d, (), (0, -d), ALL, low)
        out["QZ", d, 1] = ("z", d, (), (-d, 0), ALL, high)
    for d in (1, -1):
        out["PZ", d, 1, 0] = ("z", d, (), (-d, 0), ALL, low)
        out["QY1", d, 0] = ("y", d, (), (0, -d), ALL, high)
    for d in (1, -1):
        out["PY2", d] = ("y", d, (("PY1", d),), (0, -2 * d), HALF[d], low)
    first = {-1: (("PY1", 1),), 1: (("PY1", -1),), 2: (("PY2", 1), ("PY2", -1))}
    for o in (0, -1, 1, 2):
        for d in (1, -1):
            for t in (1, 2, 3, 4):
                if (o, t) == (0, 1):
                    continue
                parents = first[o] if t == 1 else (("PZ", d, t - 1, o),)
                out["PZ", d, t, o] = ("z", d, parents, (-t * d, o), HALF[d] if t == 4 else ALL, low)
    for d in (1, -1):
        for t in (2, 3, 4):
            blocks = HALF[d] if t == 4 else ALL
            out["QZ", d, t] = ("z", d, (("QZ", d, t - 1),), (-t * d, 0), blocks, high)
    for oz in (0, -1, 1, -2, 2, -3, 3, 4):
        for d in (1, -1):
            if oz == 4:
                parents = (("QZ", 1, 4), ("QZ", -1, 4))
            else:
                parents = (("QZ", 1 if oz < 0 else -1, abs(oz)),)
            if oz:
                out["QY1", d, oz] = ("y", d, parents, (oz, -d), ALL, high)
            out["QY2", d, oz] = ("y", d, (("QY1", d, oz),), (oz, -2 * d), HALF[d], high)
    return out


def rows_in(message):
    (b0, b1), (lo, hi) = message[4:6]
    return (b1 - b0) * (hi - lo)


RATE, HOP = 46e3, 1.7
GATHER_AHEAD, REDUCE_AHEAD = 1.5, 1.5


class Model:
    def __init__(self, messages, back):
        self.messages, self.back = messages, back
        self.ahead = REDUCE_AHEAD if back else GATHER_AHEAD
        self.took = {key: rows_in(m) * WIDE * 2 / RATE for key, m in messages.items()}
        self.after = {key: [k for k, m in messages.items() if key in m[2]] for key in messages}
        self.links = {m[:2]: 0.0 for m in messages.values()}
        self.landed, self.got, self.flying, self.program = set(), set(), [], []
        self.now, self.weight = 0.0, {}
        self.open, self.waiting = set(), {(c, key) for c in (0, 1) for key in messages}

    def needs(self, key):
        if self.back:
            return self.after[key]
        return self.messages[key][2]

    def path(self, key):
        if key not in self.weight:
            nexts = self.messages[key][2] if self.back else self.after[key]
            self.weight[key] = self.took[key] + HOP + max([self.path(k) for k in nexts] + [0.0])
        return self.weight[key]

    def land(self):
        while self.flying and self.flying[0][0] <= self.now + 1e-9:
            _, _, c, key = heapq.heappop(self.flying)
            self.landed.add((c, key))
            twin = (c, (key[0], -key[1]) + key[2:])
            if twin in self.landed:
                self.got |= {(c, key), twin}
                if not self.back:
                    self.program.append(("recv", c, key))
                    self.now += 0.03

    def send(self):
        best = None
        for c, key in self.waiting:
            link = self.messages[key][:2]
            if c in self.open and self.links[link] - self.ahead <= self.now + 1e-9:
                if all((c, k) in self.got for k in self.needs(key)):
                    rank = (c, -self.path(key), NUMBER[key])
                    if best is None or rank < best[0]:
                        best = (rank, c, key, link)
        if best is None:
            return False
        _, c, key, link = best
        self.waiting.remove((c, key))
        if self.back:
            self.now += 0.05 + self.took[key] * 0.08
        self.links[link] = max(self.now, self.links[link]) + self.took[key]
        heapq.heappush(self.flying, (self.links[link] + HOP, len(self.program), c, key))
        self.program.append(("send", c, key))
        return True

    def run(self, timed, spare):
        last, timed, spare = 0.0, list(timed(self)), list(spare(self))
        while True:
            self.land()
            if self.send():
                continue
            times = [f[0] for f in self.flying[:1]]
            times += [self.links[self.messages[k][:2]] - self.ahead for c, k in self.waiting
                      if c in self.open and all((c, n) in self.got for n in self.needs(k))]
            soon = min([t for t in times if t > self.now] + [1e9])
            if timed and timed[0][3](self) and last + timed[0][2] <= self.now + 1e-9:
                name, cost = timed.pop(0)[:2]
            elif spare and spare[0][2](self) and soon - self.now >= 0.5 * spare[0][1]:
                name, cost = spare.pop(0)[:2]
            else:
                if timed and timed[0][3](self):
                    soon = min(soon, max(last + timed[0][2], self.now + 1e-6))
                if soon > 1e8:
                    return self.program
                self.now = soon
                continue
            self.program.append(("fill",) + name)
            self.now += cost
            if not spare or name[0] not in ("turn", "edge"):
                last = self.now
            if name == ("gate",):
                self.open.add(1)


def gather_program(messages):
    model = Model(messages, False)
    model.open = {0, 1}
    full = lambda m: sum(1 for c, _ in m.got if c == 0) == len(messages)
    timed = [(("sum", n), 0.12, 0.0, full) for n in range(32)]
    timed += [(("far",), 0.2, 1.0, full), (("early",), 0.2, 0.0, full),
              (("near",), 0.2, 3.0, full), (("end",), 0.2, 4.0, full)]
    started = lambda m: m.now > 3.0
    spare = [(("turn", n), 0.12, started) for n in range(CAP + 1)]
    return model.run(lambda m: timed, lambda m: spare), model.now


def reduce_program(messages):
    model = Model(messages, True)
    model.open = {0}
    always = lambda m: True
    timed = [(("share_near",), 0.1, 1.0, always), (("weights", 0), 0.5, 0.0, always),
             (("share_far",), 0.1, 3.5, always), (("share_end",), 0.1, 1.5, always)]
    timed += [(("term", n), 0.4, 0.0, always) for n in range(CAP // 8)] + [(("gate",), 0.0, 0.0, always)]
    timed += [(("weights", n), 0.3, 0.0 if n == 1 else 3.5, always) for n in range(1, 6)]
    opened = lambda m: 1 in m.open
    spare = [(("edge", n), 0.1, opened) for n in range(CAP)]
    return model.run(lambda m: timed, lambda m: spare), model.now


MESSAGES = plane_messages()
NUMBER = {key: i for i, key in enumerate(MESSAGES)}
GATHER, SPAN = gather_program(MESSAGES)
REDUCE, BACK = reduce_program(MESSAGES)
TWIN = {key: (key[0], -key[1]) + key[2:] for key in MESSAGES}
PAIR = {key: NUMBER[key if key[1] > 0 else TWIN[key]] for key in MESSAGES}
COUNT = len(MESSAGES)
OFFSET = {}
_total = 0
for _key, _m in MESSAGES.items():
    OFFSET[_key] = _total
    _total += rows_in(_m)
PLANE_ROWS = _total
SLOT = {key: sorted(set(PAIR.values())).index(PAIR[key]) for key in MESSAGES}
CHILDREN = {key: [k for k, m in MESSAGES.items() if key in m[2]] for key in MESSAGES}
ROOTS = [k for k, m in MESSAGES.items() if not m[2]]


def kernel(
    tab, bias_in, mask_in, feats_in, w_msg_in, w_self_in, gout_in, edges,
    hidden, gfeats, EB, wgrad, bgrad,
    bias, mask, feats, w_msg, w_self, gout, HF0, HF1,
    F0, F1, A, AT, U0, U1, SS0, SS1, SR0, SR1, H0, H1,
    XS0, XS1, XR0, XR1, CS, RX0, RX1, RR0, RR1, SO, SH, GP, GW,
    WC, WR, ZS, ZR, YR, ZG, CG, ACC, MASK,
    loc, ag_s, ag_r, rs_s, rs_r, x_s, x_r, h_s, h_r, w_s, w_r,
):
    F, U, SS, SR, H = (F0, F1), (U0, U1), (SS0, SS1), (SR0, SR1), (H0, H1)
    HF = (HF0, HF1)
    XS, XR, RX, RR = (XS0, XS1), (XR0, XR1), (RX0, RX1), (RR0, RR1)
    row = lax.axis_index("row")
    col = lax.axis_index("col")
    z, y = row // NY, row % NY
    x, core = col // 2, col % 2
    other = 1 - core

    def plane_device(dz, dy):
        return ((z + dz) % NZ * NY + (y + dy) % NY, col)

    def col_device(dx, swap=False):
        return (row, (x + dx) % NX * 2 + (other if swap else core))

    def remote(src, dst, ssem, rsem, device):
        return pltpu.make_async_remote_copy(
            src_ref=src, dst_ref=dst, send_sem=ssem, recv_sem=rsem,
            device_id=device, device_id_type=MESH,
        )

    def rows_of(start, size, step=16):
        return pl.ds(pl.multiple_of(start, step), size)

    edge_in = pltpu.make_async_copy(edges, A, loc.at[0])
    loads = [
        pltpu.make_async_copy(src, dst, loc.at[i + 1])
        for i, (src, dst) in enumerate((
            (feats_in, feats), (mask_in, mask), (w_msg_in, w_msg), (w_self_in, w_self),
            (gout_in, gout), (bias_in, bias),
        ))
    ]
    for load in loads[:2]:
        load.start()
    edge_in.start()
    for load in loads[2:]:
        load.start()
    barrier = pltpu.get_barrier_semaphore()
    peers = [plane_device(0, 1), plane_device(0, -1), plane_device(1, 0), plane_device(-1, 0)]
    peers += [col_device(1), col_device(-1), col_device(0, True)]
    for peer in peers:
        pl.semaphore_signal(barrier, inc=1, device_id=peer, device_id_type=MESH)
    for load in loads[:2]:
        load.wait()
    flags = mask[...].astype(F32)
    for n in range(4):
        real = jnp.broadcast_to(flags[n:n + 1, :], (BLK, BLK)).T
        MASK[n * BLK:(n + 1) * BLK, :] = real
        for c in (0, 1):
            f = feats[n * BLK:(n + 1) * BLK, c * WIDE:(c + 1) * WIDE]
            F[c][row * 4 + n] = f * real.astype(BF)
    for c in (0, 1):
        F[c][TCOLS] = jnp.zeros((BLK, WIDE), BF)
        U[c][CAP] = jnp.zeros((BLK, WIDE), BF)

    pl.semaphore_wait(barrier, len(peers))

    gathers = {}

    def gather_copy(c, key):
        if (c, key) not in gathers:
            axis, d, _, (dz, dy), (b0, b1), (lo, hi) = MESSAGES[key]
            sz, sy = (dz + d, dy) if axis == "z" else (dz, dy + d)
            block = (z + sz) % NZ * NY + (y + sy) % NY
            part = F[c].at[pl.ds(block * 4 + b0, b1 - b0), pl.ds(lo, hi - lo), :]
            target = plane_device(d, 0) if axis == "z" else plane_device(0, d)
            gathers[c, key] = remote(part, part, ag_s.at[c], ag_r.at[c, SLOT[key]], target)
        return gathers[c, key]

    def pair_wait(c, sem, key):
        part = SR[c].at[pl.ds(0, 2 * rows_in(MESSAGES[key])), :]
        pltpu.make_async_copy(part, part, sem.at[c, SLOT[key]]).wait()

    def transpose_slot(j):
        def run():
            AT[j] = A[tab[0, PERM + j]].astype(F32).T.astype(BF)
        return run

    def sum_block(c, owner, j, dest, place):
        l = owner * 4 + j
        acc = None
        for k in range(3):
            s = k * TROWS + l
            d = jnp.dot(A[s], F[c][tab[0, FIDX + s]], preferred_element_type=F32)
            acc = d if acc is None else acc + d
        dest[rows_of(place * OWN + j * BLK, BLK, BLK), :] = acc.astype(dest.dtype)

    swaps = {}

    def swap_copy(c, rel):
        if (c, rel) not in swaps:
            part = rows_of((x + rel) % NX * OWN, OWN)
            swaps[c, rel] = remote(
                XS[c].at[part, :], XR[c].at[part, :], x_s.at[c], x_r.at[c * 10 + rel],
                col_device(0, True),
            )
        return swaps[c, rel]

    rings = {}
    RING = {
        ("F", 1): (0, 256), ("F", -1): (256, 256), ("E", 1): (512, 256), ("E", -1): (768, 256),
        ("L", 1): (1024, 256), ("L", -1): (1280, 256),
    }

    def ring_copy(c, key):
        if (c, key) not in rings:
            lo, size = RING[key]
            i = c * 10 + 4 + list(RING).index(key)
            rings[c, key] = remote(
                RX[c].at[pl.ds(lo, size), :], RR[c].at[pl.ds(lo, size), :],
                x_s.at[2 + c], x_r.at[i], col_device(-key[1]),
            )
        return rings[c, key]

    def chip_sum(c, xi, lo, size):
        part = rows_of(xi * OWN + lo, size)
        return CS[part, :] + XR[c][part, :].astype(F32)

    def ring_far(c):
        swap_copy(c, 2).wait_recv()
        for d in (1, -1):
            lo, size = RING["F", d]
            RX[c][pl.ds(lo, size), :] = chip_sum(
                c, (x + 2) % NX, 0 if d > 0 else 256, 256).astype(BF)
            ring_copy(c, ("F", d)).start()

    def ring_early(c):
        for d in (1, -1):
            swap_copy(c, 3 if d > 0 else 1).wait_recv()
            lo, size = RING["E", d]
            RX[c][pl.ds(lo, size), :] = chip_sum(
                c, (x - d) % NX, 256 if d > 0 else 0, 256).astype(BF)
            ring_copy(c, ("E", d)).start()

    def ring_near(c):
        for d in (1, -1):
            ring_copy(c, ("F", d)).wait_recv()
            lo, size = RING["L", d]
            value = chip_sum(c, (x - d) % NX, 0 if d > 0 else 256, 256)
            value = value + RR[c][pl.ds(RING["F", d][0], 256), :].astype(F32)
            RX[c][pl.ds(lo, size), :] = value.astype(BF)
            ring_copy(c, ("L", d)).start()

    def ring_end(c):
        swap_copy(c, 0).wait_recv()
        for half in (0, 1):
            now, old = (("L", 1), ("E", -1)) if half == 0 else (("L", -1), ("E", 1))
            value = chip_sum(c, x, half * 256, 256)
            for key in (old, now):
                ring_copy(c, key).wait_recv()
                value = value + RR[c][pl.ds(RING[key][0], 256), :].astype(F32)
            SO[half * 256:(half + 1) * 256, c * WIDE:(c + 1) * WIDE] = value

    TURN = (2, 1, 3, 0)

    def sum_slot(c, n):
        rel, j = TURN[n % 16 // 4], n % 4
        xi = (x + rel) % NX
        if n < 16:
            sum_block(c, 2 * xi + other, j, XS[c], xi)
            if j == 3:
                swap_copy(c, rel).start()
        else:
            sum_block(c, 2 * xi + core, j, CS, xi)

    def sum_group(c, rel, mine):
        xi = (x + rel) % NX

        for j in range(4):
            if mine:
                sum_block(c, 2 * xi + core, j, CS, xi)
            else:
                sum_block(c, 2 * xi + other, j, XS[c], xi)

    def turn(n):
        if n == 0:
            edge_in.wait()
            for load in loads[2:]:
                load.wait()
        else:
            transpose_slot(n - 1)()

    gather_steps = {
        "turn": turn, "sum": lambda n: sum_slot(0, n), "far": lambda: ring_far(0),
        "early": lambda: ring_early(0), "near": lambda: ring_near(0), "end": lambda: ring_end(0),
    }
    for step, *what in GATHER:
        if step == "send":
            gather_copy(*what).start()
        elif step == "recv":
            pair_wait(what[0], ag_r, what[1])
        else:
            gather_steps[what[0]](*what[1:])

    for rel in TURN:
        sum_group(1, rel, False)
        swap_copy(1, rel).start()
    sum_group(1, 2, True)
    ring_far(1)
    sum_group(1, 1, True)
    sum_group(1, 3, True)
    ring_early(1)
    sum_group(1, 0, True)
    ring_near(1)
    ring_end(1)

    T_DIM = (((1,), (1,)), ((), ()))
    C_DIM = (((0,), (0,)), ((), ()))

    for i in range(4):
        part = pl.ds(i * BLK, BLK)
        s = SO[part, :]
        hi = s.astype(BF)
        lo = (s - hi.astype(F32)).astype(BF)
        SH[part, :] = hi
        mine = row * 4 + i
        pre = jnp.dot(hi, w_msg[...], preferred_element_type=F32)
        pre += jnp.dot(lo, w_msg[...], preferred_element_type=F32)
        pre += jnp.dot(F0[mine], w_self[:WIDE, :], preferred_element_type=F32)
        pre += jnp.dot(F1[mine], w_self[WIDE:, :], preferred_element_type=F32)
        pre += bias[...]
        real = jnp.concatenate([MASK[part, :], MASK[part, :]], axis=1)
        sig = jax.nn.sigmoid(pre)
        hidden[part, :] = (pre * sig * real).astype(BF)
        deriv = sig * (1.0 + pre * (1.0 - sig))
        gp = (gout[part, :].astype(F32) * real * deriv).astype(BF)
        GP[part, :] = gp
        h = lax.dot_general(gp, w_msg[...], T_DIM, preferred_element_type=F32).astype(BF)
        H0[col * 4 + i] = h[:, :WIDE]
        H1[col * 4 + i] = h[:, WIDE:]

    shares = {}
    SHARE = {
        ("X1", 1): (0, 1, False, -1, 0, 4), ("X1", -1): (1, -1, False, 1, 0, 4),
        ("X2", 1): (2, 1, False, -2, 0, 2), ("X2", -1): (3, -1, False, 2, 2, 2),
        ("S", 0): (4, 0, True, 0, 0, 4), ("S", -1): (5, 0, True, -1, 0, 4),
        ("S", 1): (6, 0, True, 1, 0, 4),
        ("S", 2): (7, 0, True, 2, 0, 2), ("S", 3): (8, 0, True, 2, 2, 2),
    }

    def share_copy(c, key):
        if (c, key) not in shares:
            i, dx, swap, origin, lo, size = SHARE[key]
            from_x = origin if swap else origin + dx
            block = (x + from_x) % NX * 2 + core
            part = H[c].at[pl.ds(block * 4 + lo, size)]
            land = part
            if key[0] == "X2" or lo + size != 4 or key[1] == 3:
                land = HF[c].at[pl.ds(core * 4 + lo, size)]
            if key[0] == "S" and key[1] in (2, 3):
                part = land
            i += 9 * c
            shares[c, key] = remote(part, land, h_s.at[c], h_r.at[i], col_device(dx, swap))
        return shares[c, key]

    def share_start(c):
        for key in (("X1", 1), ("X1", -1), ("S", 0)):
            share_copy(c, key).start()

    def share_near(c):
        for d in (1, -1):
            share_copy(c, ("X1", d)).wait_recv()
            share_copy(c, ("X2", d)).start()
            share_copy(c, ("S", -d)).start()

    def share_far(c):
        for d in (1, -1):
            share_copy(c, ("X2", d)).wait_recv()
            share_copy(c, ("S", 2 if d > 0 else 3)).start()

    def share_end(c, which):
        for n in which:
            share_copy(c, ("S", n)).wait_recv()
        if 3 in which:
            for n in range(8):
                H[c][(x + 2) % NX * 8 + n] = HF[c][n]

    def term_slots(c, start, count, acc, late=False, size=12):
        def body(n, acc):
            for u in range(size):
                j = start + n * size + u
                h = HF[c][tab[0, PROW + j] & 7] if late else H[c][tab[0, PROW + j]]
                at = AT[j]
                keep = tab[0, SAME + j].astype(F32)
                acc = acc * keep + jnp.dot(at, h, preferred_element_type=F32)
                U[c][j] = acc.astype(BF)
            return acc
        return body(0, acc) if count == size else lax.fori_loop(0, count // size, body, acc)

    share_start(0)

    WG = WC

    @pl.loop(0, 1)
    def _(i):
        gp = GP[...]
        w1 = lax.dot_general(SH[...], gp, C_DIM, preferred_element_type=F32)
        for n in range(4):
            WG[n, 0:64, :] = w1[n * 64:(n + 1) * 64]
        for c in (0, 1):
            fc = F[c][pl.ds(row * 4, 4)].reshape(OWN, WIDE)
            w2 = lax.dot_general(fc, gp, C_DIM, preferred_element_type=F32)
            for n in range(2):
                WG[4 + 2 * c + n, 0:64, :] = w2[n * 64:(n + 1) * 64]
        b = jnp.sum(gp.astype(F32).reshape(64, 8, FEAT), axis=0)
        for n in range(8):
            WG[n, 64:72, :] = b
        GW[...] = lax.dot_general(gp, w_self[...], T_DIM, preferred_element_type=F32)

    share_near(0)
    share_start(1)
    share_end(0, (0, -1, 1))
    zero = jnp.zeros((BLK, WIDE), F32)
    acc = term_slots(0, 0, 36, zero)
    share_far(0)
    term_slots(0, 36, NEAR - 36, acc)
    share_end(0, (2, 3))
    term_slots(0, NEAR, CAP - NEAR, zero, late=True)

    STAGES = {"col": (0, NC, WR), "z": (1, NZ, ZR), "y": (2, NY, YR), "zg": (3, NZ, ZG), "cg": (4, NC, CG)}

    def stage_send(kind):
        i, n, _ = STAGES[kind]
        for d in range(1, n):
            to_col, to_z = (col + d) % NC, (z + d) % NZ
            src, dst, device = {
                "col": (WC.at[to_col], WR.at[col], (row, to_col)),
                "z": (ZS.at[to_z], ZR.at[z], plane_device(d, 0)),
                "y": (YR.at[y], YR.at[y], plane_device(0, d)),
                "zg": (ZG.at[z], ZG.at[z], plane_device(d, 0)),
                "cg": (CG.at[col], CG.at[col], (row, to_col)),
            }[kind]
            remote(src, dst, w_s.at[i], w_r.at[i], device).start()

    def stage_wait(kind, sems=None):
        i, n, buf = STAGES[kind]
        part = buf.at[pl.ds(0, n - 1)]
        pltpu.make_async_copy(part, part, (w_r if sems is None else sems).at[i]).wait()

    def weights_0():
        WR[col] = WC[col]
        stage_send("col")

    def weights_1():
        stage_wait("col")
        v = WR[0]
        for n in range(1, NC):
            v = v + WR[n]
        for n in range(NZ):
            ZS[n] = jnp.concatenate([v[n * 8:n * 8 + 8], v[64:72]], axis=0).astype(BF)
        ZR[z] = ZS[z]
        stage_send("z")

    def weights_2():
        stage_wait("z")
        v = ZR[0].astype(F32)
        for n in range(1, NZ):
            v = v + ZR[n].astype(F32)
        YR[y] = v.astype(BF)
        stage_send("y")

    def weights_3():
        stage_wait("y")
        v = YR[0].astype(F32)
        for n in range(1, NY):
            v = v + YR[n].astype(F32)
        ZG[z] = v[0:8].astype(BF)
        bgrad[...] = jnp.sum(v[8:16], axis=0, keepdims=True) * FACTOR
        stage_send("zg")

    def weights_4():
        stage_wait("zg")
        for n in range(NZ):
            CG[col, n * 8:n * 8 + 8, :] = ZG[n]
        stage_send("cg")

    def weights_5():
        stage_wait("cg")
        for n in range(NC):
            wgrad[n * 64:(n + 1) * 64, :] = CG[n].astype(F32) * FACTOR

    reduces = {}

    def reduce_copy(c, key):
        if (c, key) not in reduces:
            axis, d = MESSAGES[key][:2]
            part = pl.ds(OFFSET[key], rows_in(MESSAGES[key]))
            target = plane_device(-d, 0) if axis == "z" else plane_device(0, -d)
            reduces[c, key] = remote(
                SS[c].at[part, :], SR[c].at[part, :], rs_s.at[c], rs_r.at[c, SLOT[key]], target)
        return reduces[c, key]

    def total_piece(c, block, n, lo, hi, children):
        m = UIDX + block * 4 + n
        value = U[c][tab[0, m], lo:hi, :].astype(F32) + U[c][tab[0, m + TCOLS], lo:hi, :].astype(F32)
        for k in children:
            (b0, b1), rows = MESSAGES[k][4:6]
            if rows == (lo, hi) and b0 <= n < b1:
                at = OFFSET[k] + (n - b0) * (hi - lo)
                value = value + SR[c][pl.ds(at, hi - lo), :].astype(F32)
        return value

    waited = set()

    def reduce_wait(c, keys):
        for k in keys:
            if (c, k) not in waited:
                waited.add((c, k))
                waited.add((c, TWIN[k]))
                pair_wait(c, rs_r, k)

    def reduce_send(c, key):
        _, _, _, (dz, dy), (b0, b1), (lo, hi) = MESSAGES[key]
        children = CHILDREN[key]
        reduce_wait(c, children)
        block = (z + dz) % NZ * NY + (y + dy) % NY
        for n in range(b0, b1):
            at = OFFSET[key] + (n - b0) * (hi - lo)
            SS[c][pl.ds(at, hi - lo), :] = total_piece(c, block, n, lo, hi, children).astype(BF)
        reduce_copy(c, key).start()

    def finish(c):
        reduce_wait(c, ROOTS)
        part = slice(c * WIDE, (c + 1) * WIDE)
        for n in range(4):
            for lo, hi in ((0, CUT), (CUT, BLK)):
                a, b = n * BLK + lo, n * BLK + hi
                value = total_piece(c, row, n, lo, hi, ROOTS) * MASK[a:b, :]
                gfeats[a:b, part] = (value + GW[a:b, part]).astype(BF)

    def edge_slot(s):
        def run():
            e = None
            for c in (0, 1):
                f = F[c][tab[0, FIDX + s]]
                d = lax.dot_general(H[c][s % TROWS], f, T_DIM, preferred_element_type=F32)
                e = d if e is None else e + d
            EB[s] = e.astype(BF)
        return run

    def term_filler(n):
        acc = zero if n * 8 in (0, NEAR) else ACC[...]
        ACC[...] = term_slots(1, n * 8, 8, acc, size=8)

    weights = (weights_0, weights_1, weights_2, weights_3, weights_4, weights_5)
    reduce_steps = {
        "share_near": lambda: share_near(1), "share_far": lambda: share_far(1),
        "share_end": lambda: share_end(1, (0, -1, 1, 2, 3)), "gate": lambda: None,
        "weights": lambda n: weights[n](), "term": term_filler, "edge": lambda n: edge_slot(n)(),
    }
    for step, *what in REDUCE:
        if step == "send":
            reduce_send(*what)
        else:
            reduce_steps[what[0]](*what[1:])
    finish(0)
    finish(1)
    for kind in STAGES:
        stage_wait(kind, w_s)
    for c in (0, 1):
        near = H[c].at[pl.ds(0, 28)]
        pltpu.make_async_copy(near, near, h_s.at[c]).wait()
        pltpu.make_async_copy(XS[c], XS[c], x_s.at[c]).wait()
        pltpu.make_async_copy(RX[c], RX[c], x_s.at[2 + c]).wait()
        pltpu.make_async_copy(SS[c], SS[c], ag_s.at[c]).wait()
        pltpu.make_async_copy(SS[c], SS[c], rs_s.at[c]).wait()


def run_kernel(tab, bias, mask, feats, w_msg, w_self, gout, edges):
    vm = pl.BlockSpec(memory_space=pltpu.VMEM)
    dma = pltpu.SemaphoreType.DMA
    b16 = lambda rows: pltpu.VMEM((rows, WIDE), BF)
    f32 = lambda *shape: pltpu.VMEM(shape, F32)
    half = lambda *shape: pltpu.VMEM(shape, BF)
    blocks = lambda n: pltpu.VMEM((n, BLK, WIDE), BF)
    edge_shape = jax.ShapeDtypeStruct((CAP, BLK, BLK), BF)
    scratch = [
        f32(1, FEAT), pltpu.VMEM((4, BLK), jnp.int32), pltpu.VMEM((OWN, FEAT), BF),
        pltpu.VMEM((FEAT, FEAT), BF), pltpu.VMEM((FEAT, FEAT), BF), pltpu.VMEM((OWN, FEAT), BF),
        pltpu.VMEM((8, BLK, WIDE), BF), pltpu.VMEM((8, BLK, WIDE), BF),
        blocks(TCOLS + 1), blocks(TCOLS + 1), blocks(CAP), blocks(CAP),
        blocks(CAP + 1), blocks(CAP + 1),
        b16(PLANE_ROWS), b16(PLANE_ROWS), b16(PLANE_ROWS), b16(PLANE_ROWS),
        blocks(TROWS), blocks(TROWS),
        b16(NX * OWN), b16(NX * OWN), b16(NX * OWN), b16(NX * OWN), f32(NX * OWN, WIDE),
        b16(1536), b16(1536), b16(1536), b16(1536),
        f32(OWN, FEAT), pltpu.VMEM((OWN, FEAT), BF), pltpu.VMEM((OWN, FEAT), BF), f32(OWN, FEAT),
        f32(NC, 72, FEAT), f32(NC, 72, FEAT), half(NZ, 16, FEAT), half(NZ, 16, FEAT),
        half(NY, 16, FEAT), half(NZ, 8, FEAT), half(NC, 64, FEAT), f32(BLK, WIDE), f32(OWN, WIDE),
        dma((7,)), dma((2,)), dma((2, COUNT // 2)), dma((2,)), dma((2, COUNT // 2)),
        dma((4,)), dma((20,)), dma((2,)), dma((18,)), dma((5,)), dma((5,)),
    ]
    return pl.pallas_call(
        kernel,
        out_shape=(
            jax.ShapeDtypeStruct((OWN, FEAT), BF),
            jax.ShapeDtypeStruct((OWN, FEAT), BF),
            edge_shape,
            jax.ShapeDtypeStruct((2 * FEAT, FEAT), F32),
            jax.ShapeDtypeStruct((1, FEAT), F32),
        ),
        in_specs=[pl.BlockSpec(memory_space=pltpu.SMEM)]
        + [pl.BlockSpec(memory_space=pltpu.HBM)] * 7,
        out_specs=(vm,) * 5,
        scratch_shapes=scratch,
        compiler_params=pltpu.CompilerParams(
            collective_id=0, has_side_effects=True, vmem_limit_bytes=48 * 1024 * 1024
        ),
    )(tab, *[pltpu.with_memory_space_constraint(v, pltpu.HBM)
             for v in (bias, mask, feats, w_msg, w_self, gout, edges)])


def hand_over(hidden, gfeats, edge, wgrad, bgrad):
    def body(h_in, g_in, e_in, w_in, b_in, h, g, e, w1, w2, b, sem):
        copies = [
            pltpu.make_async_copy(src, dst, sem.at[i]) for i, (src, dst) in enumerate((
                (e_in, e), (h_in, h), (g_in, g), (w_in.at[pl.ds(0, FEAT)], w1),
                (w_in.at[pl.ds(FEAT, FEAT)], w2), (b_in, b),
            ))
        ]
        for copy in copies:
            copy.start()
        for copy in copies:
            copy.wait()

    like = lambda shape, dtype: jax.ShapeDtypeStruct(shape, dtype)
    return pl.pallas_call(
        body,
        out_shape=(
            like((OWN, FEAT), BF), like((OWN, FEAT), BF), like((CAP, BLK, BLK), BF),
            like((FEAT, FEAT), F32), like((FEAT, FEAT), F32), like((1, FEAT), F32),
        ),
        in_specs=[pl.BlockSpec(memory_space=pltpu.VMEM)] * 5,
        out_specs=[pl.BlockSpec(memory_space=pl.ANY)] * 6,
        scratch_shapes=[pltpu.SemaphoreType.DMA((6,))],
        compiler_params=pltpu.CompilerParams(vmem_limit_bytes=8 * 1024 * 1024),
    )(hidden, gfeats, edge, wgrad, bgrad)


def slot_tables(cols, count, far):
    s = jnp.arange(CAP, dtype=jnp.int32)
    key = jnp.where(s < count, cols, TCOLS)
    late = s % TROWS // 8 == far
    order = key + jnp.where(late, TCOLS + 1, 0)
    before = (order[None, :] == order[:, None]) & (s[None, :] < s[:, None])
    rank = jnp.sum(((order[None, :] < order[:, None]) | before).astype(jnp.int32), axis=1)
    again = jnp.any(before, axis=1).astype(jnp.int32)
    place = (rank[None, :] == s[:, None]).astype(jnp.int32)
    perm = jnp.sum(place * s[None, :], axis=1)
    same = jnp.sum(place * again[None, :], axis=1)
    m = jnp.arange(2 * TCOLS, dtype=jnp.int32)
    want = m + jnp.where(m < TCOLS, 0, 1)
    last = jnp.max(jnp.where(order[None, :] == want[:, None], rank[None, :], -1), axis=1)
    uidx = jnp.where(last < 0, CAP, last)
    return jnp.concatenate([key, perm, perm % TROWS, same, uidx])[None, :]


def per_device(feats, w_msg, w_self, bias, hit_mask, block_cols, block_count, edge_vals, grad_out):
    far = (lax.axis_index("col") // 2 + 2) % NX
    tab = slot_tables(block_cols[0, 0], block_count[0, 0], far)
    hidden, gfeats, edge, wgrad, bgrad = run_kernel(
        tab, bias[None, :], hit_mask.reshape(4, BLK), feats, w_msg, w_self, grad_out,
        edge_vals.reshape(CAP, BLK, BLK),
    )
    hidden, gfeats, edge, g_msg, g_self, bgrad = hand_over(hidden, gfeats, edge, wgrad, bgrad)
    return (hidden, gfeats, edge.reshape(1, 1, CAP, BLK, BLK), g_msg, g_self, bgrad[0])


def solution(mesh):
    placed = (
        P(("row", "col"), None),
        P(),
        P(),
        P(),
        P(("row", "col")),
        P("row", "col", None),
        P("row", "col"),
        P("row", "col", None, None, None),
        P(("row", "col"), None),
    )
    return jax.shard_map(
        per_device,
        mesh=mesh,
        in_specs=placed,
        out_specs=(
            P(("row", "col"), None),
            P(("row", "col"), None),
            P("row", "col", None, None, None),
            P(),
            P(),
            P(),
        ),
        check_vma=False,
    )
```
